32 devices in a mesh: shard: 4 (over x, core), replica: 8 (over z, y).
Axes of the slice: x: 2, y: 2, z: 4, core: 2. Of those that a mesh axis runs over, the one named last changes fastest.
Arguments:
- gradients: bfloat16 [8, 32, 512, 512], P('replica', 'shard'), may hold values from -3 to 3
- first_moment: float32 [32, 512, 512], P(('shard', 'replica')), may hold values from -6 to 6
- second_moment: float32 [32, 512, 512], P(('shard', 'replica')), may hold values from 0.25 to 4
- left_stat: float32 [32, 512, 512], P(('shard', 'replica')), as said below
- right_stat: float32 [32, 512, 512], P(('shard', 'replica')), as said below
- left_basis: float32 [32, 512, 512], P(('shard', 'replica')), as said below
- right_basis: float32 [32, 512, 512], P(('shard', 'replica')), as said below
- refresh_flags: int32 [32], replicated, may hold values from 0 to 1, as said below
Outputs:
- direction: bfloat16 [32, 512, 512], P('shard')
- new_first: float32 [32, 512, 512], P(('shard', 'replica'))
- new_second: float32 [32, 512, 512], P(('shard', 'replica'))
- new_left: float32 [32, 512, 512], P(('shard', 'replica'))
- new_right: float32 [32, 512, 512], P(('shard', 'replica'))
- new_left_basis: float32 [32, 512, 512], P(('shard', 'replica'))
- new_right_basis: float32 [32, 512, 512], P(('shard', 'replica'))
The draws below stay inside these ranges and needn't reach their ends.
Inputs may be any that keep to these rules, and one draw needn't show every extreme that they name: Write b = ((p * 8 + q)) + j. For every q, j and k, exactly one of the two blocks with p = 2 k and p = 2 k + 1 has refresh_flags[b] = 1. `left_stat`: every block is symmetric positive definite with all eigenvalues 1 or more. `right_stat`: every block is symmetric positive definite with all eigenvalues 1 or more. `left_basis`: every block is an orthogonal matrix. `right_basis`: every block is an orthogonal matrix.
All inputs are finite; a program needn't handle non-finite values.
Results may differ from the reference program's by a relative error of at most 0.012.
Values may be sent and summed in bfloat16 or wider, within the bound.
A program may use at most 128 MiB of HBM per device.

```python
import math
import jax
import jax.numpy as jnp
from jax import lax

BLOCK = 512
BLK_DEV = 1
POWER = 2
NBLK = 32
N_SHARD = 4
N_REPLICA = 8


def definite_blocks(key):
    key_diag, key_factor = jax.random.split(key)
    diagonal = jnp.exp(jax.random.uniform(key_diag, (NBLK, BLOCK), jnp.float32, 0.0, jnp.log(10.0)))
    factor = jax.random.normal(key_factor, (NBLK, BLOCK, BLOCK), jnp.float32)
    square = jnp.einsum('kij,klj->kil', factor, factor, precision=lax.Precision.HIGHEST) * (0.5 / BLOCK)
    square = 0.5 * (square + jnp.swapaxes(square, 1, 2))
    return square + jnp.eye(BLOCK, dtype=jnp.float32)[None, :, :] * diagonal[:, :, None]


def orthogonal_blocks(key):
    matrix = jax.random.normal(key, (NBLK, BLOCK, BLOCK), jnp.float32)
    basis, upper = jnp.linalg.qr(matrix)
    return basis


def draw_left_stat(key, part):
    return definite_blocks(jax.random.fold_in(key, 101))


def draw_right_stat(key, part):
    return definite_blocks(jax.random.fold_in(key, 102))


def draw_left_basis(key, part):
    return orthogonal_blocks(jax.random.fold_in(key, 103))


def draw_right_basis(key, part):
    return orthogonal_blocks(jax.random.fold_in(key, 104))


def draw_refresh_flags(key, part):
    picks = jax.random.randint(jax.random.fold_in(key, 105), (N_SHARD // 2, N_REPLICA, BLK_DEV), 0, 2)
    shard_ids = jnp.arange(N_SHARD, dtype=jnp.int32)
    chosen = picks[shard_ids // 2]
    flagged = (chosen == (shard_ids % 2)[:, None, None]).astype(jnp.int32)
    return flagged.reshape(NBLK)


def block_scale(own_key, dims, cuts, least, high):
    level = 1.0
    for dim, blocks in cuts:
        draws = jax.random.uniform(jax.random.fold_in(jax.random.fold_in(own_key, 6), dim), (blocks,), jnp.float32, least / len(cuts), high / len(cuts))
        level = level * jnp.repeat(jnp.exp(draws), dims[dim] // blocks).reshape((-1,) + (1,) * (len(dims) - 1 - dim))
    return level


def scatter_about(stream_key, shape, width, limit, cuts=(), kind=jnp.bfloat16):
    values = width * jax.random.normal(stream_key, shape, jnp.float32)
    if cuts:
        values = values * block_scale(stream_key, shape, cuts, -0.22, 0.18)
    return jnp.clip(values, -limit, limit).astype(kind)


def setup_inputs(seed: int = 0) -> dict:
    seeds = jax.random.split(jax.random.key(seed), 9)
    gradients = scatter_about(seeds[0], (N_REPLICA, NBLK, BLOCK, BLOCK), 0.5, 3.0, ((0, 8), (1, 4)))
    first_moment = scatter_about(seeds[1], (NBLK, BLOCK, BLOCK), 1.0, 6.0, ((0, 32),), jnp.float32)
    second_moment = jnp.clip(jnp.exp(math.log(4.0) - 2.7725887 * jax.random.uniform(seeds[2], (NBLK, BLOCK, BLOCK), jnp.float32) ** block_scale(seeds[2], (NBLK, BLOCK, BLOCK), ((0, 32),), -0.2, 0.2)), 0.25, 4.0)
    left_stat = draw_left_stat(jax.random.fold_in(seeds[8], 71), 0)
    right_stat = draw_right_stat(jax.random.fold_in(seeds[8], 71), 0)
    left_basis = draw_left_basis(jax.random.fold_in(seeds[8], 71), 0)
    right_basis = draw_right_basis(jax.random.fold_in(seeds[8], 71), 0)
    refresh_flags = draw_refresh_flags(jax.random.fold_in(seeds[8], 71), 0)
    return dict(gradients=gradients, first_moment=first_moment, second_moment=second_moment, left_stat=left_stat, right_stat=right_stat, left_basis=left_basis, right_basis=right_basis, refresh_flags=refresh_flags)


beta_one = 0.95
beta_two = 0.95
epsilon = 1e-08
bias_step = 10.0

def highest(left_side, right_side):
    return jnp.dot(left_side.astype(jnp.float32), right_side.astype(jnp.float32), precision=lax.Precision.HIGHEST, preferred_element_type=jnp.float32)

def orthonormal(matrix):
    gram = highest(matrix.T, matrix)
    lower_factor = jnp.linalg.cholesky(gram)
    return jax.scipy.linalg.solve_triangular(lower_factor, matrix.T, lower=True).T

def power_step(factor, basis):
    for repeat in range(POWER):
        product = jnp.dot(factor.astype(jnp.bfloat16).astype(jnp.float32), basis.astype(jnp.bfloat16).astype(jnp.float32), preferred_element_type=jnp.float32)
        basis = orthonormal(product)
    return basis

def update_block(grad_stack, moment, second, left_factor, right_factor, basis_old_left, basis_old_right, flagged):
    summed = lax.optimization_barrier(jnp.sum(grad_stack.astype(jnp.float32), axis=0))
    low_grad = summed.astype(jnp.bfloat16)
    left_new = beta_two * left_factor + (1.0 - beta_two) / BLOCK * jnp.dot(low_grad.astype(jnp.float32), low_grad.T.astype(jnp.float32), preferred_element_type=jnp.float32)
    right_new = beta_two * right_factor + (1.0 - beta_two) / BLOCK * jnp.dot(low_grad.T.astype(jnp.float32), low_grad.astype(jnp.float32), preferred_element_type=jnp.float32)

    def refresh_both():
        basis_left = power_step(left_new, basis_old_left)
        basis_right = power_step(right_new, basis_old_right)
        carried = highest(highest(highest(basis_left.T, basis_old_left), moment), highest(basis_old_right.T, basis_right))
        return (basis_left, basis_right, carried)

    def retain():
        return (basis_old_left, basis_old_right, moment)
    basis_left, basis_right, carried = lax.cond(flagged == 1, refresh_both, retain)
    rotated = highest(highest(basis_left.T, summed), basis_right)
    moment_new = beta_one * carried + (1.0 - beta_one) * rotated
    second_new = beta_two * second + (1.0 - beta_two) * rotated * rotated
    scaled = moment_new / (1.0 - beta_one ** bias_step) / (jnp.sqrt(second_new / (1.0 - beta_two ** bias_step)) + epsilon)
    direction = highest(highest(basis_left, scaled), basis_right.T).astype(jnp.bfloat16)
    return (direction, moment_new, second_new, left_new, right_new, basis_left, basis_right)

def reference(gradients, first_moment, second_moment, left_stat, right_stat, left_basis, right_basis, refresh_flags):

    def handle(position):
        pieces = [lax.dynamic_index_in_dim(array, position, 0, keepdims=False) for array in (first_moment, second_moment, left_stat, right_stat, left_basis, right_basis)]
        grad_stack = lax.dynamic_index_in_dim(gradients, position, 1, keepdims=False)
        flagged = lax.dynamic_index_in_dim(refresh_flags, position, 0, keepdims=False)
        return update_block(grad_stack, pieces[0], pieces[1], pieces[2], pieces[3], pieces[4], pieces[5], flagged)
    results = lax.map(handle, jnp.arange(NBLK, dtype=jnp.int32))
    return (results[0], results[1], results[2], results[3], results[4], results[5], results[6])
```

```python
import jax
import jax.numpy as jnp
from jax import lax
from jax.experimental import pallas as pl
from jax.experimental.pallas import tpu as pltpu
from jax.sharding import PartitionSpec as P

POWER = 2


beta_one = 0.95
beta_two = 0.95
epsilon = 1e-08
bias_step = 10.0

TILE = 128
ROWS = 8
CHUNKS = 4
MESH = pl.DeviceIdType.MESH


def paired(block):
    count = lax.axis_size("shard")
    return lax.ppermute(block, "shard", [(low, low ^ 1) for low in range(count)])


def product(left_side, right_side, contract=(1, 0), precision=lax.Precision.HIGHEST):
    return lax.dot_general(
        left_side,
        right_side,
        (((contract[0],), (contract[1],)), ((), ())),
        precision=precision,
        preferred_element_type=jnp.float32,
    )


def low_product(left_side, right_side, contract=(1, 0)):
    return product(
        left_side.astype(jnp.bfloat16), right_side.astype(jnp.bfloat16), contract, None
    )


HEAD = 8


def spread_lane(rows, at):
    return jnp.broadcast_to(rows[:, at : at + 1], rows.shape) + 0.0

def spread_row(rows, at):
    return jnp.broadcast_to(rows[at : at + 1, :], rows.shape)

def inverse_factor(tile):
    side = tile.shape[0]
    spread = (ROWS, side)
    lane = lax.broadcasted_iota(jnp.int32, spread, 1)
    sub = lax.broadcasted_iota(jnp.int32, spread, 0)
    parts = HEAD // ROWS
    count = side // HEAD
    groups = [tile[ROWS * g : ROWS * (g + 1), :] for g in range(side // ROWS)]
    finished = []
    for step in range(count):
        start = HEAD * step
        first = parts * step
        inside = (lane >= start) & (lane < start + HEAD)
        old = groups[first : first + parts]
        columns = [[spread_lane(rows, start + t) for rows in old] for t in range(HEAD)]
        lines = [
            jnp.where(inside, jnp.where(lane == start + ROWS * v + sub, 1.0, 0.0), old[v])
            for v in range(parts)
        ]
        done = [jnp.zeros(spread, jnp.float32)] * parts
        scale = [jnp.zeros(spread, jnp.float32)] * parts
        for j in range(HEAD):
            own, row = divmod(j, ROWS)
            here = sub == row
            pivot = spread_row(columns[j][own], row)
            inverse = 1.0 / pivot
            ratio = [column * inverse for column in columns[j]]
            ratio[own] = jnp.where(here, 0.0, ratio[own])
            for t in range(j + 1, HEAD):
                across = spread_row(columns[j][t // ROWS], t % ROWS)
                for v in range(parts):
                    if t == j + 1:
                        change = (columns[j][v] * across) * inverse
                        if v == own:
                            change = jnp.where(here, 0.0, change)
                    else:
                        change = ratio[v] * across
                    columns[t][v] = columns[t][v] - change
            line = spread_row(lines[own], row)
            done[own] = jnp.where(here, line * lax.rsqrt(pivot), done[own])
            scale[own] = jnp.where(here, inverse, scale[own])
            for v in range(parts):
                lines[v] = lines[v] - ratio[v] * line
        finished += [jnp.where(lane < start + HEAD, rows, 0.0) for rows in done]
        if step + 1 == count:
            break
        back = [lines[v] * scale[v] for v in range(parts)]
        edge = min(first + parts, side // ROWS)
        across = [spread_row(back[j // ROWS], j % ROWS) for j in range(HEAD)]
        for g in range(first + parts, edge):
            terms = [spread_lane(groups[g], start + j) * across[j] for j in range(HEAD)]
            while len(terms) > 1:
                terms = [terms[t] + terms[t + 1] for t in range(0, len(terms), 2)]
            groups[g] = jnp.where(inside, 0.0, groups[g]) - terms[0]
        if edge < side // ROWS:
            change = lax.dot_general(wide(jnp.concatenate(old, 0), 0), wide(jnp.concatenate(back, 0), 1), (((0,), (0,)), ((), ())), preferred_element_type=jnp.float32)
            for g in range(edge, side // ROWS):
                groups[g] = jnp.where(inside, 0.0, groups[g]) - change[ROWS * g : ROWS * (g + 1), :]
    return jnp.concatenate(finished, 0)

def wide(x, kind):
    a = x.astype(jnp.bfloat16); r = x - a.astype(jnp.float32); b = r.astype(jnp.bfloat16); c = (r - b.astype(jnp.float32)).astype(jnp.bfloat16)
    return jnp.concatenate([a, a, b, b, a, c] if kind == 0 else [a, b, a, b, c, a], 0)


def refresh_kernel(listed_ref, left_ref, left_basis_ref, incoming_ref, turned_ref, basis_ref, held, joint):
    side = left_ref.shape[0]
    listed = listed_ref[0] == 1

    @pl.when(listed)
    def _():
        held[...] = left_basis_ref[...].T

    @pl.when(jnp.logical_not(listed))
    def _():
        held[...] = incoming_ref[1].astype(jnp.float32).T

    factor = jnp.where(
        jnp.full((side, side), listed_ref[0], jnp.int32) == 1,
        left_ref[...].astype(jnp.float32),
        incoming_ref[0].astype(jnp.float32),
    ).astype(jnp.bfloat16)
    turned_ref[...] = factor

    def repeat(_, carry):
        turned = product(held[...].astype(jnp.bfloat16), turned_ref[...], precision=None)
        joint[:, side:] = turned
        joint[:, :side] = product(turned, turned, (1, 1))

        tile = joint[:TILE, :TILE]
        for block in range(side // TILE):
            at, after = block * TILE, (block + 1) * TILE
            inverse = inverse_factor(tile)
            if after < side:
                near = product(joint[after : after + TILE, at:after], inverse, (1, 1))
                tile = joint[after : after + TILE, after : after + TILE] - product(
                    near, near, (1, 1)
                )
            fresh = product(inverse, joint[at:after, side:])
            held[at:after, :] = fresh
            if after < side:
                joint[after : after + TILE, side:] -= product(near, fresh)
            if after + TILE < side:
                below = product(joint[after + TILE :, at:after], inverse, (1, 1))
                joint[after + TILE :, after : after + TILE] -= product(below, near, (1, 1))
                joint[after + TILE :, after + TILE : side] -= product(below, below, (1, 1))
                joint[after + TILE :, side:] -= product(below, fresh)
        return carry

    lax.fori_loop(0, POWER, repeat, 0)
    turned_ref[...] = held[...].T.astype(jnp.bfloat16)

    @pl.when(listed)
    def _():
        basis_ref[...] = held[...].T

    @pl.when(jnp.logical_not(listed))
    def _():
        basis_ref[...] = left_basis_ref[...]


def statistics_kernel(grad_ref, left_ref, right_ref, basis_ref, left_out, right_out, low_out, send_out):
    grad = grad_ref[...]
    rate = (1.0 - beta_two) / grad.shape[0]
    left = beta_two * left_ref[...] + rate * low_product(grad, grad, (1, 1))
    left_out[...] = left
    low_out[...] = left.astype(jnp.bfloat16)
    right = beta_two * right_ref[...] + rate * low_product(grad, grad, (0, 0))
    right_out[...] = right
    send_out[0] = right.astype(jnp.bfloat16)
    send_out[1] = basis_ref[...].astype(jnp.bfloat16)


def update_kernel(
    listed_ref,
    grad_ref,
    moment_ref,
    second_ref,
    old_left_ref,
    old_right_ref,
    left_ref,
    arrived_ref,
    moment_out,
    second_out,
    right_out,
    direction_out,
):
    listed = listed_ref[0] == 1

    @pl.when(listed)
    def _():
        right_out[...] = arrived_ref[...].astype(jnp.float32)
        plain = low_product(
            low_product(old_left_ref[...], moment_ref[...]), old_right_ref[...], (1, 1)
        )
        moment_out[...] = low_product(
            low_product(left_ref[...], plain, (0, 0)), arrived_ref[...]
        )

    @pl.when(jnp.logical_not(listed))
    def _():
        right_out[...] = old_right_ref[...]
        moment_out[...] = moment_ref[...]

    left = left_ref[...].astype(jnp.bfloat16)
    right = right_out[...].astype(jnp.bfloat16)
    rotated = low_product(low_product(left, grad_ref[...], (0, 0)), right)
    moment_new = beta_one * moment_out[...] + (1.0 - beta_one) * rotated
    second_new = beta_two * second_ref[...] + (1.0 - beta_two) * rotated * rotated
    moment_out[...] = moment_new
    second_out[...] = second_new
    scaled = (
        moment_new
        / (1.0 - beta_one**bias_step)
        / (jnp.sqrt(second_new / (1.0 - beta_two**bias_step)) + epsilon)
    )
    direction_out[...] = low_product(low_product(left, scaled), right, (1, 1)).astype(
        jnp.bfloat16
    )


def sequence(outer_count):
    return sorted(range(outer_count), key=lambda m: (m == 0, abs(2 * m - outer_count), m))


def place(outer_count):
    me = lax.axis_index("replica")
    inner = lax.rem(me, 2)
    return me, inner, me // 2, me + 1 - 2 * inner


def meet(outer_count):
    me, inner, outer, partner = place(outer_count)
    barrier = pltpu.get_barrier_semaphore()
    pl.semaphore_signal(barrier, inc=1, device_id={"replica": partner}, device_id_type=MESH)
    for m in range(1, outer_count):
        other = lax.rem(outer + m, outer_count) * 2 + inner
        pl.semaphore_signal(barrier, inc=1, device_id={"replica": other}, device_id_type=MESH)
    pl.semaphore_wait(barrier, outer_count)


def remote(source, target, send_sem, recv_sem, replica):
    return pltpu.make_async_remote_copy(
        src_ref=source,
        dst_ref=target,
        send_sem=send_sem,
        recv_sem=recv_sem,
        device_id={"replica": replica},
        device_id_type=MESH,
    )


def sum_kernel(
    grad_ref, out_ref, mine, got, pairs, far, load_sem, near_send, near_recv, far_send, far_recv
):
    outer_count = mine.shape[0]
    rows = mine.shape[1] // CHUNKS
    me, inner, outer, partner = place(outer_count)
    meet(outer_count)
    order = sequence(outer_count)
    near, loads = {}, {}
    for m in order:
        aim = lax.rem(outer + m, outer_count)
        for c in range(CHUNKS):
            part = pl.ds(c * rows, rows)
            near[m, c] = remote(
                grad_ref.at[0, aim * 2 + 1 - inner, part],
                got.at[m, part],
                near_send.at[m, c],
                near_recv.at[m, c],
                partner,
            )
            near[m, c].start()
        loads[m] = pltpu.make_async_copy(
            grad_ref.at[0, aim * 2 + inner], mine.at[m], load_sem.at[m]
        )
        loads[m].start()
    away = {}
    for m in order:
        aim = lax.rem(outer + m, outer_count)
        loads[m].wait()
        for c in range(CHUNKS):
            part = pl.ds(c * rows, rows)
            near[m, c].wait_recv()
            total = mine[m, part].astype(jnp.float32) + got[m, part].astype(jnp.float32)
            if m != 0:
                pairs[m, part] = total.astype(jnp.bfloat16)
                away[m, c] = remote(
                    pairs.at[m, part],
                    far.at[m, part],
                    far_send.at[m, c],
                    far_recv.at[m, c],
                    aim * 2 + inner,
                )
                away[m, c].start()
    for c in range(CHUNKS):
        part = pl.ds(c * rows, rows)
        total = mine[0, part].astype(jnp.float32) + got[0, part].astype(jnp.float32)
        for m in order[:-1]:
            away[m, c].wait_recv()
            total = total + far[m, part].astype(jnp.float32)
        out_ref[part] = total.astype(jnp.bfloat16)
    for copy in list(near.values()) + list(away.values()):
        copy.wait_send()


def gather_kernel(
    block_ref, out_ref, own_sem, near_send, near_recv, up_send, up_recv, down_send, down_recv
):
    outer_count = out_ref.shape[0] // 2
    rows = block_ref.shape[0] // CHUNKS
    me, inner, outer, partner = place(outer_count)
    meet(outer_count)
    keep = pltpu.make_async_copy(block_ref, out_ref.at[me], own_sem.at[0])
    keep.start()

    def above():
        return outer + 1 < outer_count

    def below():
        return outer >= 1

    def move(kind, distance, c):
        part = pl.ds(c * rows, rows)
        if kind == "up":
            sems, target, origin = (up_send, up_recv), me + 2, me - 2 * distance
        elif kind == "down":
            sems, target, origin = (down_send, down_recv), me - 2, me + 2 * distance
        else:
            sems, target, origin = (near_send, near_recv), partner, me + 2 * distance
        slot = distance + outer_count - 1 if kind == "near" else distance
        source = block_ref.at[part] if distance == 0 else out_ref.at[origin, part]
        return remote(
            source, out_ref.at[origin, part], sems[0].at[slot, c], sems[1].at[slot, c], target
        )

    for c in range(CHUNKS):
        pl.when(above())(move("up", 0, c).start)
        pl.when(below())(move("down", 0, c).start)
    for c in range(CHUNKS):
        move("near", 0, c).start()
    for distance in range(1, outer_count):
        for c in range(CHUNKS):

            @pl.when(outer >= distance)
            def _():
                move("up", distance - 1, c).wait_recv()
                pl.when(above())(move("up", distance, c).start)
                move("near", -distance, c).start()

            @pl.when(outer + distance < outer_count)
            def _():
                move("down", distance - 1, c).wait_recv()
                pl.when(below())(move("down", distance, c).start)
                move("near", distance, c).start()

    for distance in range(outer_count):
        for c in range(CHUNKS):

            @pl.when(outer >= distance)
            def _():
                move("near", -distance, c).wait()
                pl.when(above())(move("up", distance, c).wait_send)

            @pl.when(outer + distance < outer_count)
            def _():
                if distance:
                    move("near", distance, c).wait()
                pl.when(below())(move("down", distance, c).wait_send)

    keep.wait()


VMEM = pl.BlockSpec(memory_space=pltpu.VMEM)
SMEM = pl.BlockSpec(memory_space=pltpu.SMEM)
ANY = pl.BlockSpec(memory_space=pl.ANY)


def replica_sum(gradients):
    count, side = gradients.shape[1], gradients.shape[2]
    outer = count // 2
    held = pltpu.VMEM((outer, side, side), jnp.bfloat16)
    flags = pltpu.SemaphoreType.DMA((outer, CHUNKS))
    return pl.pallas_call(
        sum_kernel,
        out_shape=jax.ShapeDtypeStruct((side, side), jnp.bfloat16),
        in_specs=[ANY],
        out_specs=VMEM,
        scratch_shapes=[held] * 4 + [pltpu.SemaphoreType.DMA((outer,))] + [flags] * 4,
        compiler_params=pltpu.CompilerParams(collective_id=0, has_side_effects=True),
        name="replica_sum",
    )(gradients)


def replica_gather(block, count):
    side = block.shape[0]
    outer = count // 2
    flags = pltpu.SemaphoreType.DMA((outer, CHUNKS))
    wide = pltpu.SemaphoreType.DMA((2 * outer - 1, CHUNKS))
    return pl.pallas_call(
        gather_kernel,
        out_shape=jax.ShapeDtypeStruct((count, side, side), jnp.bfloat16),
        in_specs=[VMEM],
        out_specs=ANY,
        scratch_shapes=[pltpu.SemaphoreType.DMA((1,))] + [wide] * 2 + [flags] * 4,
        compiler_params=pltpu.CompilerParams(collective_id=1, has_side_effects=True),
        name="replica_gather",
    )(block)


def local(
    gradients,
    first_moment,
    second_moment,
    left_stat,
    right_stat,
    left_basis,
    right_basis,
    refresh_flags,
):
    replica_count = lax.axis_size("replica")
    owner_id = lax.axis_index("shard") * replica_count + lax.axis_index("replica")
    listed = lax.dynamic_slice_in_dim(refresh_flags, owner_id, 1)
    side = left_stat.shape[1]
    wide = jax.ShapeDtypeStruct((side, side), jnp.float32)
    low = jax.ShapeDtypeStruct((side, side), jnp.bfloat16)
    low_grad = replica_sum(gradients)
    left_new, right_new, left_low, outgoing = pl.pallas_call(
        statistics_kernel,
        out_shape=(wide, wide, low, jax.ShapeDtypeStruct((2, side, side), jnp.bfloat16)),
        in_specs=[VMEM] * 4,
        out_specs=(VMEM,) * 4,
        name="statistics",
    )(low_grad, left_stat[0], right_stat[0], right_basis[0])
    incoming = paired(outgoing)
    turned, new_left = pl.pallas_call(
        refresh_kernel,
        out_shape=(low, wide),
        in_specs=[SMEM] + [VMEM] * 3,
        out_specs=(VMEM,) * 2,
        scratch_shapes=[
            pltpu.VMEM((side, side), jnp.float32),
            pltpu.VMEM((side, 2 * side), jnp.float32),
        ],
        name="refresh",
    )(listed, left_low, left_basis[0], incoming)
    arrived = paired(turned)
    moment_new, second_new, new_right, outward = pl.pallas_call(
        update_kernel,
        out_shape=(wide, wide, wide, low),
        in_specs=[SMEM] + [VMEM] * 7,
        out_specs=(VMEM,) * 4,
        name="update",
    )(
        listed,
        low_grad,
        first_moment[0],
        second_moment[0],
        left_basis[0],
        right_basis[0],
        new_left,
        arrived,
    )
    gathered = replica_gather(outward, replica_count)
    return (
        gathered,
        moment_new[None],
        second_new[None],
        left_new[None],
        right_new[None],
        new_left[None],
        new_right[None],
    )


def solution(mesh):
    owned = P(("shard", "replica"), None, None)
    in_specs = (P("replica", "shard", None, None),) + (owned,) * 6 + (P(),)
    out_specs = (P("shard", None, None),) + (owned,) * 6
    return jax.shard_map(local, mesh=mesh, in_specs=in_specs, out_specs=out_specs, check_vma=False)
```

```python
import jax
import jax.numpy as jnp
from jax import lax
from jax.experimental import pallas as pl
from jax.experimental.pallas import tpu as pltpu
from jax.sharding import PartitionSpec as P

POWER = 2


beta_one = 0.95
beta_two = 0.95
epsilon = 1e-08
bias_step = 10.0

TILE = 128
ROWS = 8
CHUNKS = 4
MESH = pl.DeviceIdType.MESH


def paired(block):
    count = lax.axis_size("shard")
    return lax.ppermute(block, "shard", [(low, low ^ 1) for low in range(count)])


def product(left_side, right_side, contract=(1, 0), precision=lax.Precision.HIGHEST):
    return lax.dot_general(
        left_side,
        right_side,
        (((contract[0],), (contract[1],)), ((), ())),
        precision=precision,
        preferred_element_type=jnp.float32,
    )


def low_product(left_side, right_side, contract=(1, 0)):
    return product(
        left_side.astype(jnp.bfloat16), right_side.astype(jnp.bfloat16), contract, None
    )


HEAD = 16


def spread_lane(rows, at):
    return jnp.broadcast_to(rows[:, at : at + 1], rows.shape) + 0.0

def spread_row(rows, at):
    return jnp.broadcast_to(rows[at : at + 1, :], rows.shape)

def inverse_factor(tile):
    side = tile.shape[0]
    spread = (ROWS, side)
    lane = lax.broadcasted_iota(jnp.int32, spread, 1)
    sub = lax.broadcasted_iota(jnp.int32, spread, 0)
    parts = HEAD // ROWS
    count = side // HEAD
    groups = [tile[ROWS * g : ROWS * (g + 1), :] for g in range(side // ROWS)]
    finished = []
    for step in range(count):
        start = HEAD * step
        first = parts * step
        inside = (lane >= start) & (lane < start + HEAD)
        old = groups[first : first + parts]
        columns = [[spread_lane(rows, start + t) for rows in old] for t in range(HEAD)]
        lines = [
            jnp.where(inside, jnp.where(lane == start + ROWS * v + sub, 1.0, 0.0), old[v])
            for v in range(parts)
        ]
        done = [jnp.zeros(spread, jnp.float32)] * parts
        scale = [jnp.zeros(spread, jnp.float32)] * parts
        for j in range(HEAD):
            own, row = divmod(j, ROWS)
            here = sub == row
            pivot = spread_row(columns[j][own], row)
            inverse = 1.0 / pivot
            ratio = [column * inverse for column in columns[j]]
            ratio[own] = jnp.where(here, 0.0, ratio[own])
            for t in range(j + 1, HEAD):
                across = spread_row(columns[j][t // ROWS], t % ROWS)
                for v in range(parts):
                    if t == j + 1:
                        change = (columns[j][v] * across) * inverse
                        if v == own:
                            change = jnp.where(here, 0.0, change)
                    else:
                        change = ratio[v] * across
                    columns[t][v] = columns[t][v] - change
            line = spread_row(lines[own], row)
            done[own] = jnp.where(here, line * lax.rsqrt(pivot), done[own])
            scale[own] = jnp.where(here, inverse, scale[own])
            for v in range(parts):
                lines[v] = lines[v] - ratio[v] * line
        finished += [jnp.where(lane < start + HEAD, rows, 0.0) for rows in done]
        if step + 1 == count:
            break
        back = [lines[v] * scale[v] for v in range(parts)]
        edge = min(first + 2 * parts, side // ROWS)
        across = [spread_row(back[j // ROWS], j % ROWS) for j in range(HEAD)]
        for g in range(first + parts, edge):
            terms = [spread_lane(groups[g], start + j) * across[j] for j in range(HEAD)]
            while len(terms) > 1:
                terms = [terms[t] + terms[t + 1] for t in range(0, len(terms), 2)]
            groups[g] = jnp.where(inside, 0.0, groups[g]) - terms[0]
        if edge < side // ROWS:
            change = lax.dot_general(wide(jnp.concatenate(old, 0), 0), wide(jnp.concatenate(back, 0), 1), (((0,), (0,)), ((), ())), preferred_element_type=jnp.float32)
            for g in range(edge, side // ROWS):
                groups[g] = jnp.where(inside, 0.0, groups[g]) - change[ROWS * g : ROWS * (g + 1), :]
    return jnp.concatenate(finished, 0)

def wide(x, kind):
    a = x.astype(jnp.bfloat16); r = x - a.astype(jnp.float32); b = r.astype(jnp.bfloat16); c = (r - b.astype(jnp.float32)).astype(jnp.bfloat16)
    return jnp.concatenate([a, a, b, b, a, c] if kind == 0 else [a, b, a, b, c, a], 0)


def refresh_kernel(listed_ref, left_ref, left_basis_ref, incoming_ref, turned_ref, basis_ref, held, joint):
    side = left_ref.shape[0]
    listed = listed_ref[0] == 1

    @pl.when(listed)
    def _():
        held[...] = left_basis_ref[...].T

    @pl.when(jnp.logical_not(listed))
    def _():
        held[...] = incoming_ref[1].astype(jnp.float32).T

    factor = jnp.where(
        jnp.full((side, side), listed_ref[0], jnp.int32) == 1,
        left_ref[...].astype(jnp.float32),
        incoming_ref[0].astype(jnp.float32),
    ).astype(jnp.bfloat16)
    turned_ref[...] = factor

    def repeat(_, carry):
        turned = product(held[...].astype(jnp.bfloat16), turned_ref[...], precision=None)
        joint[:, side:] = turned
        joint[:, :side] = product(turned, turned, (1, 1))

        tile = joint[:TILE, :TILE]
        for block in range(side // TILE):
            at, after = block * TILE, (block + 1) * TILE
            inverse = inverse_factor(tile)
            if after < side:
                near = product(joint[after : after + TILE, at:after], inverse, (1, 1))
                tile = joint[after : after + TILE, after : after + TILE] - product(
                    near, near, (1, 1)
                )
            fresh = product(inverse, joint[at:after, side:])
            held[at:after, :] = fresh
            if after < side:
                joint[after : after + TILE, side:] -= product(near, fresh)
            if after + TILE < side:
                below = product(joint[after + TILE :, at:after], inverse, (1, 1))
                joint[after + TILE :, after : after + TILE] -= product(below, near, (1, 1))
                joint[after + TILE :, after + TILE : side] -= product(below, below, (1, 1))
                joint[after + TILE :, side:] -= product(below, fresh)
        return carry

    lax.fori_loop(0, POWER, repeat, 0)
    turned_ref[...] = held[...].T.astype(jnp.bfloat16)

    @pl.when(listed)
    def _():
        basis_ref[...] = held[...].T

    @pl.when(jnp.logical_not(listed))
    def _():
        basis_ref[...] = left_basis_ref[...]


def statistics_kernel(grad_ref, left_ref, right_ref, basis_ref, left_out, right_out, low_out, send_out):
    grad = grad_ref[...]
    rate = (1.0 - beta_two) / grad.shape[0]
    left = beta_two * left_ref[...] + rate * low_product(grad, grad, (1, 1))
    left_out[...] = left
    low_out[...] = left.astype(jnp.bfloat16)
    right = beta_two * right_ref[...] + rate * low_product(grad, grad, (0, 0))
    right_out[...] = right
    send_out[0] = right.astype(jnp.bfloat16)
    send_out[1] = basis_ref[...].astype(jnp.bfloat16)


def update_kernel(
    listed_ref,
    grad_ref,
    moment_ref,
    second_ref,
    old_left_ref,
    old_right_ref,
    left_ref,
    arrived_ref,
    moment_out,
    second_out,
    right_out,
    direction_out,
):
    listed = listed_ref[0] == 1

    @pl.when(listed)
    def _():
        right_out[...] = arrived_ref[...].astype(jnp.float32)
        plain = low_product(
            low_product(old_left_ref[...], moment_ref[...]), old_right_ref[...], (1, 1)
        )
        moment_out[...] = low_product(
            low_product(left_ref[...], plain, (0, 0)), arrived_ref[...]
        )

    @pl.when(jnp.logical_not(listed))
    def _():
        right_out[...] = old_right_ref[...]
        moment_out[...] = moment_ref[...]

    left = left_ref[...].astype(jnp.bfloat16)
    right = right_out[...].astype(jnp.bfloat16)
    rotated = low_product(low_product(left, grad_ref[...], (0, 0)), right)
    moment_new = beta_one * moment_out[...] + (1.0 - beta_one) * rotated
    second_new = beta_two * second_ref[...] + (1.0 - beta_two) * rotated * rotated
    moment_out[...] = moment_new
    second_out[...] = second_new
    scaled = (
        moment_new
        / (1.0 - beta_one**bias_step)
        / (jnp.sqrt(second_new / (1.0 - beta_two**bias_step)) + epsilon)
    )
    direction_out[...] = low_product(low_product(left, scaled), right, (1, 1)).astype(
        jnp.bfloat16
    )


def sequence(outer_count):
    return sorted(range(outer_count), key=lambda m: (m == 0, abs(2 * m - outer_count), m))


def place(outer_count):
    me = lax.axis_index("replica")
    inner = lax.rem(me, 2)
    return me, inner, me // 2, me + 1 - 2 * inner


def meet(outer_count):
    me, inner, outer, partner = place(outer_count)
    barrier = pltpu.get_barrier_semaphore()
    pl.semaphore_signal(barrier, inc=1, device_id={"replica": partner}, device_id_type=MESH)
    for m in range(1, outer_count):
        other = lax.rem(outer + m, outer_count) * 2 + inner
        pl.semaphore_signal(barrier, inc=1, device_id={"replica": other}, device_id_type=MESH)
    pl.semaphore_wait(barrier, outer_count)


def remote(source, target, send_sem, recv_sem, replica):
    return pltpu.make_async_remote_copy(
        src_ref=source,
        dst_ref=target,
        send_sem=send_sem,
        recv_sem=recv_sem,
        device_id={"replica": replica},
        device_id_type=MESH,
    )


def sum_kernel(
    grad_ref, out_ref, mine, got, pairs, far, load_sem, near_send, near_recv, far_send, far_recv
):
    outer_count = mine.shape[0]
    rows = mine.shape[1] // CHUNKS
    me, inner, outer, partner = place(outer_count)
    meet(outer_count)
    order = sequence(outer_count)
    near, loads = {}, {}
    for m in order:
        aim = lax.rem(outer + m, outer_count)
        for c in range(CHUNKS):
            part = pl.ds(c * rows, rows)
            near[m, c] = remote(
                grad_ref.at[0, aim * 2 + 1 - inner, part],
                got.at[m, part],
                near_send.at[m, c],
                near_recv.at[m, c],
                partner,
            )
            near[m, c].start()
        loads[m] = pltpu.make_async_copy(
            grad_ref.at[0, aim * 2 + inner], mine.at[m], load_sem.at[m]
        )
        loads[m].start()
    away = {}
    for m in order:
        aim = lax.rem(outer + m, outer_count)
        loads[m].wait()
        for c in range(CHUNKS):
            part = pl.ds(c * rows, rows)
            near[m, c].wait_recv()
            total = mine[m, part].astype(jnp.float32) + got[m, part].astype(jnp.float32)
            if m != 0:
                pairs[m, part] = total.astype(jnp.bfloat16)
                away[m, c] = remote(
                    pairs.at[m, part],
                    far.at[m, part],
                    far_send.at[m, c],
                    far_recv.at[m, c],
                    aim * 2 + inner,
                )
                away[m, c].start()
    for c in range(CHUNKS):
        part = pl.ds(c * rows, rows)
        total = mine[0, part].astype(jnp.float32) + got[0, part].astype(jnp.float32)
        for m in order[:-1]:
            away[m, c].wait_recv()
            total = total + far[m, part].astype(jnp.float32)
        out_ref[part] = total.astype(jnp.bfloat16)
    for copy in list(near.values()) + list(away.values()):
        copy.wait_send()


def gather_kernel(
    block_ref, out_ref, own_sem, near_send, near_recv, up_send, up_recv, down_send, down_recv
):
    outer_count = out_ref.shape[0] // 2
    rows = block_ref.shape[0] // CHUNKS
    me, inner, outer, partner = place(outer_count)
    meet(outer_count)
    keep = pltpu.make_async_copy(block_ref, out_ref.at[me], own_sem.at[0])
    keep.start()

    def above():
        return outer + 1 < outer_count

    def below():
        return outer >= 1

    def move(kind, distance, c):
        part = pl.ds(c * rows, rows)
        if kind == "up":
            sems, target, origin = (up_send, up_recv), me + 2, me - 2 * distance
        elif kind == "down":
            sems, target, origin = (down_send, down_recv), me - 2, me + 2 * distance
        else:
            sems, target, origin = (near_send, near_recv), partner, me + 2 * distance
        slot = distance + outer_count - 1 if kind == "near" else distance
        source = block_ref.at[part] if distance == 0 else out_ref.at[origin, part]
        return remote(
            source, out_ref.at[origin, part], sems[0].at[slot, c], sems[1].at[slot, c], target
        )

    for c in range(CHUNKS):
        pl.when(above())(move("up", 0, c).start)
        pl.when(below())(move("down", 0, c).start)
    for c in range(CHUNKS):
        move("near", 0, c).start()
    for distance in range(1, outer_count):
        for c in range(CHUNKS):

            @pl.when(outer >= distance)
            def _():
                move("up", distance - 1, c).wait_recv()
                pl.when(above())(move("up", distance, c).start)
                move("near", -distance, c).start()

            @pl.when(outer + distance < outer_count)
            def _():
                move("down", distance - 1, c).wait_recv()
                pl.when(below())(move("down", distance, c).start)
                move("near", distance, c).start()

    for distance in range(outer_count):
        for c in range(CHUNKS):

            @pl.when(outer >= distance)
            def _():
                move("near", -distance, c).wait()
                pl.when(above())(move("up", distance, c).wait_send)

            @pl.when(outer + distance < outer_count)
            def _():
                if distance:
                    move("near", distance, c).wait()
                pl.when(below())(move("down", distance, c).wait_send)

    keep.wait()


VMEM = pl.BlockSpec(memory_space=pltpu.VMEM)
SMEM = pl.BlockSpec(memory_space=pltpu.SMEM)
ANY = pl.BlockSpec(memory_space=pl.ANY)


def replica_sum(gradients):
    count, side = gradients.shape[1], gradients.shape[2]
    outer = count // 2
    held = pltpu.VMEM((outer, side, side), jnp.bfloat16)
    flags = pltpu.SemaphoreType.DMA((outer, CHUNKS))
    return pl.pallas_call(
        sum_kernel,
        out_shape=jax.ShapeDtypeStruct((side, side), jnp.bfloat16),
        in_specs=[ANY],
        out_specs=VMEM,
        scratch_shapes=[held] * 4 + [pltpu.SemaphoreType.DMA((outer,))] + [flags] * 4,
        compiler_params=pltpu.CompilerParams(collective_id=0, has_side_effects=True),
        name="replica_sum",
    )(gradients)


def replica_gather(block, count):
    side = block.shape[0]
    outer = count // 2
    flags = pltpu.SemaphoreType.DMA((outer, CHUNKS))
    wide = pltpu.SemaphoreType.DMA((2 * outer - 1, CHUNKS))
    return pl.pallas_call(
        gather_kernel,
        out_shape=jax.ShapeDtypeStruct((count, side, side), jnp.bfloat16),
        in_specs=[VMEM],
        out_specs=ANY,
        scratch_shapes=[pltpu.SemaphoreType.DMA((1,))] + [wide] * 2 + [flags] * 4,
        compiler_params=pltpu.CompilerParams(collective_id=1, has_side_effects=True),
        name="replica_gather",
    )(block)


def local(
    gradients,
    first_moment,
    second_moment,
    left_stat,
    right_stat,
    left_basis,
    right_basis,
    refresh_flags,
):
    replica_count = lax.axis_size("replica")
    owner_id = lax.axis_index("shard") * replica_count + lax.axis_index("replica")
    listed = lax.dynamic_slice_in_dim(refresh_flags, owner_id, 1)
    side = left_stat.shape[1]
    wide = jax.ShapeDtypeStruct((side, side), jnp.float32)
    low = jax.ShapeDtypeStruct((side, side), jnp.bfloat16)
    low_grad = replica_sum(gradients)
    left_new, right_new, left_low, outgoing = pl.pallas_call(
        statistics_kernel,
        out_shape=(wide, wide, low, jax.ShapeDtypeStruct((2, side, side), jnp.bfloat16)),
        in_specs=[VMEM] * 4,
        out_specs=(VMEM,) * 4,
        name="statistics",
    )(low_grad, left_stat[0], right_stat[0], right_basis[0])
    incoming = paired(outgoing)
    turned, new_left = pl.pallas_call(
        refresh_kernel,
        out_shape=(low, wide),
        in_specs=[SMEM] + [VMEM] * 3,
        out_specs=(VMEM,) * 2,
        scratch_shapes=[
            pltpu.VMEM((side, side), jnp.float32),
            pltpu.VMEM((side, 2 * side), jnp.float32),
        ],
        name="refresh",
    )(listed, left_low, left_basis[0], incoming)
    arrived = paired(turned)
    moment_new, second_new, new_right, outward = pl.pallas_call(
        update_kernel,
        out_shape=(wide, wide, wide, low),
        in_specs=[SMEM] + [VMEM] * 7,
        out_specs=(VMEM,) * 4,
        name="update",
    )(
        listed,
        low_grad,
        first_moment[0],
        second_moment[0],
        left_basis[0],
        right_basis[0],
        new_left,
        arrived,
    )
    gathered = replica_gather(outward, replica_count)
    return (
        gathered,
        moment_new[None],
        second_new[None],
        left_new[None],
        right_new[None],
        new_left[None],
        new_right[None],
    )


def solution(mesh):
    owned = P(("shard", "replica"), None, None)
    in_specs = (P("replica", "shard", None, None),) + (owned,) * 6 + (P(),)
    out_specs = (P("shard", None, None),) + (owned,) * 6
    return jax.shard_map(local, mesh=mesh, in_specs=in_specs, out_specs=out_specs, check_vma=False)
```

```python
import jax
import jax.numpy as jnp
from jax import lax
from jax.experimental import pallas as pl
from jax.experimental.pallas import tpu as pltpu
from jax.sharding import PartitionSpec as P

POWER = 2


beta_one = 0.95
beta_two = 0.95
epsilon = 1e-08
bias_step = 10.0

TILE = 128
ROWS = 8
CHUNKS = 2
MESH = pl.DeviceIdType.MESH


def product(left_side, right_side, contract=(1, 0), precision=lax.Precision.HIGHEST):
    return lax.dot_general(
        left_side,
        right_side,
        (((contract[0],), (contract[1],)), ((), ())),
        precision=precision,
        preferred_element_type=jnp.float32,
    )


def low_product(left_side, right_side, contract=(1, 0)):
    return product(
        left_side.astype(jnp.bfloat16), right_side.astype(jnp.bfloat16), contract, None
    )


HEAD = 16


def spread_lane(rows, at):
    return jnp.broadcast_to(rows[:, at : at + 1], rows.shape) + 0.0

def spread_row(rows, at):
    return jnp.broadcast_to(rows[at : at + 1, :], rows.shape)

def inverse_factor(tile):
    side = tile.shape[0]
    spread = (ROWS, side)
    lane = lax.broadcasted_iota(jnp.int32, spread, 1)
    sub = lax.broadcasted_iota(jnp.int32, spread, 0)
    parts = HEAD // ROWS
    count = side // HEAD
    groups = [tile[ROWS * g : ROWS * (g + 1), :] for g in range(side // ROWS)]
    finished = []
    for step in range(count):
        start = HEAD * step
        first = parts * step
        inside = (lane >= start) & (lane < start + HEAD)
        old = groups[first : first + parts]
        columns = [[spread_lane(rows, start + t) for rows in old] for t in range(HEAD)]
        lines = [
            jnp.where(inside, jnp.where(lane == start + ROWS * v + sub, 1.0, 0.0), old[v])
            for v in range(parts)
        ]
        done = [jnp.zeros(spread, jnp.float32)] * parts
        scale = [jnp.zeros(spread, jnp.float32)] * parts
        for j in range(HEAD):
            own, row = divmod(j, ROWS)
            here = sub == row
            pivot = spread_row(columns[j][own], row)
            inverse = 1.0 / pivot
            ratio = [column * inverse for column in columns[j]]
            ratio[own] = jnp.where(here, 0.0, ratio[own])
            for t in range(j + 1, HEAD):
                across = spread_row(columns[j][t // ROWS], t % ROWS)
                for v in range(parts):
                    if t == j + 1:
                        change = (columns[j][v] * across) * inverse
                        if v == own:
                            change = jnp.where(here, 0.0, change)
                    else:
                        change = ratio[v] * across
                    columns[t][v] = columns[t][v] - change
            line = spread_row(lines[own], row)
            done[own] = jnp.where(here, line * lax.rsqrt(pivot), done[own])
            scale[own] = jnp.where(here, inverse, scale[own])
            for v in range(parts):
                lines[v] = lines[v] - ratio[v] * line
        finished += [jnp.where(lane < start + HEAD, rows, 0.0) for rows in done]
        if step + 1 == count:
            break
        back = [lines[v] * scale[v] for v in range(parts)]
        edge = min(first + 2 * parts, side // ROWS)
        across = [spread_row(back[j // ROWS], j % ROWS) for j in range(HEAD)]
        for g in range(first + parts, edge):
            terms = [spread_lane(groups[g], start + j) * across[j] for j in range(HEAD)]
            while len(terms) > 1:
                terms = [terms[t] + terms[t + 1] for t in range(0, len(terms), 2)]
            groups[g] = jnp.where(inside, 0.0, groups[g]) - terms[0]
        if edge < side // ROWS:
            change = lax.dot_general(wide(jnp.concatenate(old, 0), 0), wide(jnp.concatenate(back, 0), 1), (((0,), (0,)), ((), ())), preferred_element_type=jnp.float32)
            for g in range(edge, side // ROWS):
                groups[g] = jnp.where(inside, 0.0, groups[g]) - change[ROWS * g : ROWS * (g + 1), :]
    return jnp.concatenate(finished, 0)

def wide(x, kind):
    a = x.astype(jnp.bfloat16); r = x - a.astype(jnp.float32); b = r.astype(jnp.bfloat16); c = (r - b.astype(jnp.float32)).astype(jnp.bfloat16)
    return jnp.concatenate([a, a, b, b, a, c] if kind == 0 else [a, b, a, b, c, a], 0)


def refresh(held, joint, turned, pauses):
    side = held.shape[0]
    steps, passed, pauses = POWER * (side // TILE), 0, list(pauses)
    spacing = len(pauses)
    for repeat in range(POWER):
        across = product(held[...].astype(jnp.bfloat16), turned[...], precision=None)
        joint[:, side:] = across
        joint[:, :side] = product(across, across, (1, 1))
        tile = joint[:TILE, :TILE]
        for block in range(side // TILE):
            at, after = block * TILE, (block + 1) * TILE
            inverse = inverse_factor(tile)
            if after < side:
                near = product(joint[after : after + TILE, at:after], inverse, (1, 1))
                tile = joint[after : after + TILE, after : after + TILE] - product(
                    near, near, (1, 1)
                )
            fresh = product(inverse, joint[at:after, side:])
            held[at:after, :] = fresh
            if after < side:
                joint[after : after + TILE, side:] -= product(near, fresh)
            if after + TILE < side:
                below = product(joint[after + TILE :, at:after], inverse, (1, 1))
                joint[after + TILE :, after : after + TILE] -= product(below, near, (1, 1))
                joint[after + TILE :, after + TILE : side] -= product(below, below, (1, 1))
                joint[after + TILE :, side:] -= product(below, fresh)
            passed += 1
            while pauses and (spacing - len(pauses) + 1) * steps <= passed * spacing:
                pauses.pop(0)()


def moved(left, right, grad, carried, second):
    rotated = low_product(low_product(left, grad, (0, 0)), right)
    moment_new = beta_one * carried + (1.0 - beta_one) * rotated
    second_new = beta_two * second + (1.0 - beta_two) * rotated * rotated
    scaled = (
        moment_new
        / (1.0 - beta_one**bias_step)
        / (jnp.sqrt(second_new / (1.0 - beta_two**bias_step)) + epsilon)
    )
    turn = low_product(low_product(left, scaled), right, (1, 1)).astype(jnp.bfloat16)
    return moment_new, second_new, turn


def sequence(outer_count):
    return sorted(range(outer_count), key=lambda m: (m == 0, abs(2 * m - outer_count), m))


def to_replica(source, target, sems, index, replica):
    return pltpu.make_async_remote_copy(
        src_ref=source,
        dst_ref=target,
        send_sem=sems.at[(0,) + index],
        recv_sem=sems.at[(1,) + index],
        device_id={"replica": replica},
        device_id_type=MESH,
    )


def to_mate(source, target, sems, index, mate):
    return pltpu.make_async_remote_copy(
        src_ref=source,
        dst_ref=target,
        send_sem=sems.at[0, index],
        recv_sem=sems.at[1, index],
        device_id={"shard": mate},
        device_id_type=MESH,
    )


def soap_kernel(
    flags_ref,
    grad_ref,
    moment_ref,
    second_ref,
    left_stat_ref,
    right_stat_ref,
    left_basis_ref,
    right_basis_ref,
    direction_out,
    moment_out,
    second_out,
    left_out,
    right_out,
    left_basis_out,
    right_basis_out,
    mine,
    inbox,
    got,
    pairs,
    far,
    sums,
    gathered,
    fresh_turn,
    mate_turn,
    own_turn,
    moment,
    second,
    left_stat,
    right_stat,
    left_basis,
    right_basis,
    mate_stat,
    mate_basis,
    own_sum,
    plain,
    turned,
    arrived,
    held,
    joint,
    load_sem,
    state_sem,
    store_sem,
    out_sem,
    swap_sem,
    mate_sem,
    give_sem,
    near_sem,
    far_sem,
    along_sem,
    across_sem,
):
    count, half, side = mine.shape
    outer_count = count // 2
    rows = half // CHUNKS
    me, shard = lax.axis_index("replica"), lax.axis_index("shard")
    core = lax.rem(shard, 2)
    mate = shard + 1 - 2 * core
    inner = lax.rem(me, 2)
    outer = me // 2
    partner = me + 1 - 2 * inner
    order = sequence(outer_count)
    listed = flags_ref[shard * count + me] == 1
    kept = pl.ds(pl.multiple_of(core * half, half), half)
    given = pl.ds(pl.multiple_of((1 - core) * half, half), half)

    def aim(m):
        return lax.rem(outer + m, outer_count)

    barrier = pltpu.get_barrier_semaphore()
    pl.semaphore_signal(barrier, inc=1, device_id={"shard": mate}, device_id_type=MESH)
    pl.semaphore_signal(barrier, inc=1, device_id={"replica": partner}, device_id_type=MESH)
    for m in range(1, outer_count):
        pl.semaphore_signal(
            barrier, inc=1, device_id={"replica": aim(m) * 2 + inner}, device_id_type=MESH
        )
    pl.semaphore_wait(barrier, outer_count + 1)

    swaps, loads = {}, {}
    for m in order:
        for k in range(2):
            owner = aim(m) * 2 + (1 - inner if k == 0 else inner)
            slot = 2 * m + k
            swaps[slot] = to_mate(
                grad_ref.at[0, owner, given], inbox.at[slot], swap_sem, slot, mate
            )
            swaps[slot].start()
            loads[slot] = pltpu.make_async_copy(
                grad_ref.at[0, owner, kept], mine.at[slot], load_sem.at[slot]
            )
            loads[slot].start()
    give_stat = to_mate(right_stat_ref.at[0], mate_stat, mate_sem, 0, mate)
    give_basis = to_mate(right_basis_ref.at[0], mate_basis, mate_sem, 1, mate)
    give_stat.start()
    give_basis.start()
    states = []
    for index, (source, target) in enumerate(
        [
            (left_stat_ref, left_stat),
            (left_basis_ref, left_basis),
            (right_stat_ref, right_stat),
            (right_basis_ref, right_basis),
            (moment_ref, moment),
            (second_ref, second),
        ]
    ):
        states.append(pltpu.make_async_copy(source.at[0], target, state_sem.at[index]))
        states[-1].start()

    def near_copy(kind, m, c):
        part = pl.ds(c * rows, rows)
        source = (mine, inbox)[kind].at[2 * m, part]
        return to_replica(source, got.at[kind, m, part], near_sem, (kind, m, c), partner)

    def far_copy(kind, m, c):
        part = pl.ds(c * rows, rows)
        return to_replica(
            pairs.at[kind, m, part],
            far.at[kind, m, part],
            far_sem,
            (kind, m, c),
            aim(m) * 2 + inner,
        )

    def own_part(kind, m, c):
        part = pl.ds(c * rows, rows)
        near_copy(kind, m, c).wait_recv()
        stay = (mine, inbox)[kind][2 * m + 1, part]
        return stay.astype(jnp.float32) + got[kind, m, part].astype(jnp.float32)

    def pass_on(kind, m):
        for c in range(CHUNKS):
            pairs[kind, m, pl.ds(c * rows, rows)] = own_part(kind, m, c).astype(jnp.bfloat16)
            far_copy(kind, m, c).start()

    def give_sum(kind, c):
        place = pl.ds(pl.multiple_of(core * half + c * rows, rows), rows)
        return to_mate(
            sums.at[kind, place], sums.at[kind, place], give_sem, kind * CHUNKS + c, mate
        )

    def finish_sum(kind, totals):
        for c in range(CHUNKS):
            part = pl.ds(c * rows, rows)
            total = totals[c]
            for m in order[:-1]:
                far_copy(kind, m, c).wait_recv()
                total = total + far[kind, m, part].astype(jnp.float32)
            place = pl.ds(pl.multiple_of(core * half + c * rows, rows), rows)
            sums[kind, place] = total.astype(jnp.bfloat16)
            give_sum(kind, c).start()

    for m in order:
        for k in range(2):
            owner = aim(m) * 2 + (1 - inner if k == 0 else inner)
            slot = 2 * m + k
            first = flags_ref[shard * count + owner] == 1
            loads[slot].wait()
            swaps[slot].wait_recv()
            one, two = mine[slot], inbox[slot]
            mine[slot] = lax.select(first, one, two)
            inbox[slot] = lax.select(first, two, one)
            if k == 0:
                for c in range(CHUNKS):
                    near_copy(0, m, c).start()
    for m in order[:-1]:
        pass_on(0, m)
    totals = [own_part(0, 0, c) for c in range(CHUNKS)]
    for m in order:
        for c in range(CHUNKS):
            near_copy(1, m, c).start()
    finish_sum(0, totals)

    for state in states[:2]:
        state.wait()
    give_stat.wait_recv()
    give_basis.wait_recv()
    held[...] = lax.select(listed, left_basis[...], mate_basis[...]).T
    for c in range(CHUNKS):
        give_sum(0, c).wait()
    grad = sums[0]
    rate = (1.0 - beta_two) / side
    turned[...] = (
        beta_two * lax.select(listed, left_stat[...], mate_stat[...])
        + rate * lax.select(listed, low_product(grad, grad, (1, 1)), low_product(grad, grad, (0, 0)))
    ).astype(jnp.bfloat16)

    def give_turn(kind):
        return to_mate(fresh_turn.at[kind, given], mate_turn.at[kind], mate_sem, 2 + kind, mate)

    def along(kind, m):
        return to_replica(
            own_turn.at[kind],
            gathered.at[kind, me],
            along_sem,
            (kind, m),
            aim(m) * 2 + inner,
        )

    def across(kind, m):
        origin = lax.rem(outer - m + outer_count, outer_count) * 2 + inner
        source = own_turn.at[kind] if m == 0 else gathered.at[kind, origin]
        return to_replica(source, gathered.at[kind, origin], across_sem, (kind, m), partner)

    def start_turn(kind, choose):
        give_turn(kind).wait()
        own_turn[kind] = lax.select(choose, fresh_turn[kind, kept], mate_turn[kind])
        for m in order[:-1]:
            along(kind, m).start()
        across(kind, 0).start()

    def forward_turn(kind):
        for m in order[:-1]:
            along(kind, m).wait_recv()
            across(kind, m).start()

    def middle():
        for state in states[2:]:
            state.wait()
        for c in range(CHUNKS):
            give_sum(1, c).wait()
        own_sum[...] = lax.select(listed, sums[0], sums[1])
        low_left, low_right = left_basis[...].astype(jnp.bfloat16), right_basis[...].astype(jnp.bfloat16)
        fresh_turn[1] = moved(low_left, low_right, own_sum[...], moment[...], second[...])[2]
        give_turn(1).start()

    def statistics():
        grad = own_sum[...]
        give_stat.wait_send()
        left_stat[...] = beta_two * left_stat[...] + rate * low_product(grad, grad, (1, 1))
        right_stat[...] = beta_two * right_stat[...] + rate * low_product(grad, grad, (0, 0))
        plain[...] = low_product(
            low_product(left_basis[...], moment[...]), right_basis[...], (1, 1)
        ).astype(jnp.bfloat16)
        store(0, left_stat, left_out).start()
        store(1, right_stat, right_out).start()

    def store(index, source, target):
        return pltpu.make_async_copy(source, target.at[0], store_sem.at[index])

    refresh(
        held,
        joint,
        turned,
        (
            lambda: pass_on(1, order[0]),
            lambda: [pass_on(1, m) for m in order[1:2]],
            lambda: [pass_on(1, m) for m in order[2:-1]],
            lambda: None,
            lambda: finish_sum(1, [own_part(1, 0, c) for c in range(CHUNKS)]),
            middle,
            lambda: [start_turn(1, jnp.logical_not(listed)), statistics()],
            lambda: None,
        ),
    )
    turned[...] = held[...].T.astype(jnp.bfloat16)
    give_turned = to_mate(turned, arrived, mate_sem, 4, mate)
    give_turned.start()
    forward_turn(1)
    left_basis[...] = lax.select(listed, held[...].T, left_basis[...])
    low_left = left_basis[...].astype(jnp.bfloat16)
    part_moment = low_product(low_left, plain[...], (0, 0))
    give_turned.wait()
    give_basis.wait_send()
    right_basis[...] = lax.select(listed, arrived[...].astype(jnp.float32), right_basis[...])
    low_right = right_basis[...].astype(jnp.bfloat16)
    carried = lax.select(listed, low_product(part_moment, low_right), moment[...])
    moment_new, second_new, turn = moved(
        low_left, low_right, own_sum[...], carried, second[...]
    )
    fresh_turn[0] = turn
    give_turn(0).start()
    moment[...] = moment_new
    second[...] = second_new
    start_turn(0, listed)
    ends = [
        store(2, moment, moment_out),
        store(3, second, second_out),
        store(4, left_basis, left_basis_out),
        store(5, right_basis, right_basis_out),
    ]
    for end in ends:
        end.start()
    ends += [store(0, left_stat, left_out), store(1, right_stat, right_out)]
    for kind in range(2):
        for m in order:
            for c in range(CHUNKS):
                near_copy(kind, m, c).wait_send()
                if m:
                    far_copy(kind, m, c).wait_send()
    for swap in swaps.values():
        swap.wait_send()

    def keep_out(owner):
        return pltpu.make_async_copy(
            mine.at[owner], direction_out.at[owner, kept], out_sem.at[owner]
        )

    def give_out(owner):
        return to_mate(
            inbox.at[owner], direction_out.at[owner, kept], swap_sem, owner, mate
        )

    def assemble(owner, first, second_kind):
        flag = flags_ref[shard * count + owner] == 1
        mine[owner] = lax.select(flag, first, second_kind)
        inbox[owner] = lax.select(flag, second_kind, first)
        keep_out(owner).start()
        give_out(owner).start()

    assemble(me, own_turn[0], own_turn[1])
    for m in order[:-1]:
        along(0, m).wait_recv()
        across(0, m).start()
        origin = lax.rem(outer - m + outer_count, outer_count) * 2 + inner
        assemble(origin, gathered[0, origin], gathered[1, origin])
    for m in (0,) + tuple(order[:-1]):
        origin = lax.rem(outer - m + outer_count, outer_count) * 2 + 1 - inner
        for kind in (1, 0):
            across(kind, m).wait_recv()
        assemble(origin, gathered[0, origin], gathered[1, origin])
    for kind in range(2):
        for m in order:
            across(kind, m).wait_send()
            if m:
                along(kind, m).wait_send()
    for end in ends:
        end.wait()
    for owner in range(count):
        keep_out(owner).wait()
        give_out(owner).wait()


SMEM = pl.BlockSpec(memory_space=pltpu.SMEM)
ANY = pl.BlockSpec(memory_space=pl.ANY)


def local(
    gradients,
    first_moment,
    second_moment,
    left_stat,
    right_stat,
    left_basis,
    right_basis,
    refresh_flags,
):
    count, side = gradients.shape[1], gradients.shape[2]
    outer, half = count // 2, side // 2
    wide = jax.ShapeDtypeStruct((1, side, side), jnp.float32)
    low = jax.ShapeDtypeStruct((count, side, side), jnp.bfloat16)

    def low_held(*shape):
        return pltpu.VMEM(shape, jnp.bfloat16)

    def flags(*shape):
        return pltpu.SemaphoreType.DMA(shape)

    block = pltpu.VMEM((side, side), jnp.float32)
    return pl.pallas_call(
        soap_kernel,
        out_shape=(low,) + (wide,) * 6,
        in_specs=[SMEM] + [ANY] * 7,
        out_specs=(ANY,) * 7,
        scratch_shapes=[
            low_held(count, half, side),
            low_held(count, half, side),
            low_held(2, outer, half, side),
            low_held(2, outer, half, side),
            low_held(2, outer, half, side),
            low_held(2, side, side),
            low_held(2, count, half, side),
            low_held(2, side, side),
            low_held(2, half, side),
            low_held(2, half, side),
        ]
        + [block] * 8
        + [low_held(side, side)] * 4
        + [block, pltpu.VMEM((side, 2 * side), jnp.float32)]
        + [
            flags(count),
            flags(6),
            flags(6),
            flags(count),
            flags(2, count),
            flags(2, 5),
            flags(2, 2 * CHUNKS),
            flags(2, 2, outer, CHUNKS),
            flags(2, 2, outer, CHUNKS),
            flags(2, 2, outer),
            flags(2, 2, outer),
        ],
        compiler_params=pltpu.CompilerParams(
            collective_id=0, has_side_effects=True, vmem_limit_bytes=60 << 20
        ),
        name="soap",
    )(
        refresh_flags,
        gradients,
        first_moment,
        second_moment,
        left_stat,
        right_stat,
        left_basis,
        right_basis,
    )


def solution(mesh):
    owned = P(("shard", "replica"), None, None)
    in_specs = (P("replica", "shard", None, None),) + (owned,) * 6 + (P(),)
    out_specs = (P("shard", None, None),) + (owned,) * 6
    return jax.shard_map(local, mesh=mesh, in_specs=in_specs, out_specs=out_specs, check_vma=False)
```

```python
import jax
import jax.numpy as jnp
from jax import lax
from jax.experimental import pallas as pl
from jax.experimental.pallas import tpu as pltpu
from jax.sharding import PartitionSpec as P

POWER = 2


beta_one = 0.95
beta_two = 0.95
epsilon = 1e-08
bias_step = 10.0

TILE = 128
ROWS = 8
CHUNKS = 4
MESH = pl.DeviceIdType.MESH


def product(left_side, right_side, contract=(1, 0), precision=lax.Precision.HIGHEST):
    return lax.dot_general(
        left_side,
        right_side,
        (((contract[0],), (contract[1],)), ((), ())),
        precision=precision,
        preferred_element_type=jnp.float32,
    )


def low_product(left_side, right_side, contract=(1, 0)):
    return product(
        left_side.astype(jnp.bfloat16), right_side.astype(jnp.bfloat16), contract, None
    )


HEAD = 16


def spread_lane(rows, at):
    return jnp.broadcast_to(rows[:, at : at + 1], rows.shape) + 0.0

def spread_row(rows, at):
    return jnp.broadcast_to(rows[at : at + 1, :], rows.shape)

def inverse_factor(tile):
    side = tile.shape[0]
    spread = (ROWS, side)
    lane = lax.broadcasted_iota(jnp.int32, spread, 1)
    sub = lax.broadcasted_iota(jnp.int32, spread, 0)
    parts = HEAD // ROWS
    count = side // HEAD
    groups = [tile[ROWS * g : ROWS * (g + 1), :] for g in range(side // ROWS)]
    finished = []
    for step in range(count):
        start = HEAD * step
        first = parts * step
        inside = (lane >= start) & (lane < start + HEAD)
        old = groups[first : first + parts]
        columns = [[spread_lane(rows, start + t) for rows in old] for t in range(HEAD)]
        lines = [
            jnp.where(inside, jnp.where(lane == start + ROWS * v + sub, 1.0, 0.0), old[v])
            for v in range(parts)
        ]
        done = [jnp.zeros(spread, jnp.float32)] * parts
        scale = [jnp.zeros(spread, jnp.float32)] * parts
        for j in range(HEAD):
            own, row = divmod(j, ROWS)
            here = sub == row
            pivot = spread_row(columns[j][own], row)
            inverse = 1.0 / pivot
            ratio = [column * inverse for column in columns[j]]
            ratio[own] = jnp.where(here, 0.0, ratio[own])
            for t in range(j + 1, HEAD):
                across = spread_row(columns[j][t // ROWS], t % ROWS)
                for v in range(parts):
                    if t == j + 1:
                        change = (columns[j][v] * across) * inverse
                        if v == own:
                            change = jnp.where(here, 0.0, change)
                    else:
                        change = ratio[v] * across
                    columns[t][v] = columns[t][v] - change
            line = spread_row(lines[own], row)
            done[own] = jnp.where(here, line * lax.rsqrt(pivot), done[own])
            scale[own] = jnp.where(here, inverse, scale[own])
            for v in range(parts):
                lines[v] = lines[v] - ratio[v] * line
        finished += [jnp.where(lane < start + HEAD, rows, 0.0) for rows in done]
        if step + 1 == count:
            break
        back = [lines[v] * scale[v] for v in range(parts)]
        edge = min(first + 2 * parts, side // ROWS)
        across = [spread_row(back[j // ROWS], j % ROWS) for j in range(HEAD)]
        for g in range(first + parts, edge):
            terms = [spread_lane(groups[g], start + j) * across[j] for j in range(HEAD)]
            while len(terms) > 1:
                terms = [terms[t] + terms[t + 1] for t in range(0, len(terms), 2)]
            groups[g] = jnp.where(inside, 0.0, groups[g]) - terms[0]
        if edge < side // ROWS:
            change = lax.dot_general(wide(jnp.concatenate(old, 0), 0), wide(jnp.concatenate(back, 0), 1), (((0,), (0,)), ((), ())), preferred_element_type=jnp.float32)
            for g in range(edge, side // ROWS):
                groups[g] = jnp.where(inside, 0.0, groups[g]) - change[ROWS * g : ROWS * (g + 1), :]
    return jnp.concatenate(finished, 0)

def wide(x, kind):
    a = x.astype(jnp.bfloat16); r = x - a.astype(jnp.float32); b = r.astype(jnp.bfloat16); c = (r - b.astype(jnp.float32)).astype(jnp.bfloat16)
    return jnp.concatenate([a, a, b, b, a, c] if kind == 0 else [a, b, a, b, c, a], 0)


def refresh(held, joint, turned, pauses):
    side = held.shape[0]
    steps, passed, pauses = POWER * (side // TILE), 0, list(pauses)
    spacing = len(pauses)
    for repeat in range(POWER):
        across = product(held[...].astype(jnp.bfloat16), turned[...], precision=None)
        joint[:, side:] = across
        joint[:, :side] = product(across, across, (1, 1))
        tile = joint[:TILE, :TILE]
        for block in range(side // TILE):
            at, after = block * TILE, (block + 1) * TILE
            inverse = inverse_factor(tile)
            if after < side:
                near = product(joint[after : after + TILE, at:after], inverse, (1, 1))
                tile = joint[after : after + TILE, after : after + TILE] - product(
                    near, near, (1, 1)
                )
            fresh = product(inverse, joint[at:after, side:])
            held[at:after, :] = fresh
            if after < side:
                joint[after : after + TILE, side:] -= product(near, fresh)
            if after + TILE < side:
                below = product(joint[after + TILE :, at:after], inverse, (1, 1))
                joint[after + TILE :, after : after + TILE] -= product(below, near, (1, 1))
                joint[after + TILE :, after + TILE : side] -= product(below, below, (1, 1))
                joint[after + TILE :, side:] -= product(below, fresh)
            passed += 1
            while pauses and (spacing - len(pauses) + 1) * steps <= passed * spacing:
                pauses.pop(0)()


def moved(left, right, grad, carried, second):
    rotated = low_product(low_product(left, grad, (0, 0)), right)
    moment_new = beta_one * carried + (1.0 - beta_one) * rotated
    second_new = beta_two * second + (1.0 - beta_two) * rotated * rotated
    scaled = (
        moment_new
        / (1.0 - beta_one**bias_step)
        / (jnp.sqrt(second_new / (1.0 - beta_two**bias_step)) + epsilon)
    )
    turn = low_product(low_product(left, scaled), right, (1, 1)).astype(jnp.bfloat16)
    return moment_new, second_new, turn


def sequence(outer_count):
    return sorted(range(outer_count), key=lambda m: (m == 0, abs(2 * m - outer_count), m))


def to_replica(source, target, sems, index, replica):
    return pltpu.make_async_remote_copy(
        src_ref=source,
        dst_ref=target,
        send_sem=sems.at[(0,) + index],
        recv_sem=sems.at[(1,) + index],
        device_id={"replica": replica},
        device_id_type=MESH,
    )


def to_mate(source, target, sems, index, mate):
    return pltpu.make_async_remote_copy(
        src_ref=source,
        dst_ref=target,
        send_sem=sems.at[0, index],
        recv_sem=sems.at[1, index],
        device_id={"shard": mate},
        device_id_type=MESH,
    )


def soap_kernel(
    flags_ref,
    grad_ref,
    moment_ref,
    second_ref,
    left_stat_ref,
    right_stat_ref,
    left_basis_ref,
    right_basis_ref,
    direction_out,
    moment_out,
    second_out,
    left_out,
    right_out,
    left_basis_out,
    right_basis_out,
    mine,
    inbox,
    got,
    pairs,
    far,
    sums,
    gathered,
    fresh_turn,
    mate_turn,
    own_turn,
    moment,
    second,
    left_stat,
    right_stat,
    left_basis,
    right_basis,
    mate_stat,
    mate_basis,
    own_sum,
    plain,
    turned,
    arrived,
    held,
    joint,
    load_sem,
    state_sem,
    store_sem,
    out_sem,
    swap_sem,
    mate_sem,
    give_sem,
    near_sem,
    far_sem,
    along_sem,
    across_sem,
):
    count, half, side = mine.shape
    outer_count = count // 2
    rows = half // CHUNKS
    me, shard = lax.axis_index("replica"), lax.axis_index("shard")
    core = lax.rem(shard, 2)
    mate = shard + 1 - 2 * core
    inner = lax.rem(me, 2)
    outer = me // 2
    partner = me + 1 - 2 * inner
    order = sequence(outer_count)
    closest = sorted(range(1, outer_count), key=lambda m: min(m, outer_count - m))
    listed = flags_ref[shard * count + me] == 1
    kept = pl.ds(pl.multiple_of(core * half, half), half)
    given = pl.ds(pl.multiple_of((1 - core) * half, half), half)

    def aim(m):
        return lax.rem(outer + m, outer_count)

    barrier = pltpu.get_barrier_semaphore()
    pl.semaphore_signal(barrier, inc=1, device_id={"shard": mate}, device_id_type=MESH)
    pl.semaphore_signal(barrier, inc=1, device_id={"replica": partner}, device_id_type=MESH)
    for m in range(1, outer_count):
        pl.semaphore_signal(
            barrier, inc=1, device_id={"replica": aim(m) * 2 + inner}, device_id_type=MESH
        )
    pl.semaphore_wait(barrier, outer_count + 1)

    swaps, loads = {}, {}
    for m in order:
        for k in range(2):
            owner = aim(m) * 2 + (1 - inner if k == 0 else inner)
            slot = 2 * m + k
            swaps[slot] = to_mate(
                grad_ref.at[0, owner, given], inbox.at[slot], swap_sem, slot, mate
            )
            swaps[slot].start()
            loads[slot] = pltpu.make_async_copy(
                grad_ref.at[0, owner, kept], mine.at[slot], load_sem.at[slot]
            )
            loads[slot].start()
    give_stat = to_mate(right_stat_ref.at[0], mate_stat, mate_sem, 0, mate)
    give_basis = to_mate(right_basis_ref.at[0], mate_basis, mate_sem, 1, mate)
    give_stat.start()
    give_basis.start()
    states = []
    for index, (source, target) in enumerate(
        [
            (left_stat_ref, left_stat),
            (left_basis_ref, left_basis),
            (right_stat_ref, right_stat),
            (right_basis_ref, right_basis),
            (moment_ref, moment),
            (second_ref, second),
        ]
    ):
        states.append(pltpu.make_async_copy(source.at[0], target, state_sem.at[index]))
        states[-1].start()

    def near_copy(kind, m, c):
        part = pl.ds(c * rows, rows)
        source = (mine, inbox)[kind].at[2 * m, part]
        return to_replica(source, got.at[kind, m, part], near_sem, (kind, m, c), partner)

    def far_copy(kind, m, c):
        part = pl.ds(c * rows, rows)
        return to_replica(
            pairs.at[kind, m, part],
            far.at[kind, m, part],
            far_sem,
            (kind, m, c),
            aim(m) * 2 + inner,
        )

    def own_part(kind, m, c):
        part = pl.ds(c * rows, rows)
        near_copy(kind, m, c).wait_recv()
        stay = (mine, inbox)[kind][2 * m + 1, part]
        return stay.astype(jnp.float32) + got[kind, m, part].astype(jnp.float32)

    def pass_on(kind, m):
        for c in range(CHUNKS):
            pairs[kind, m, pl.ds(c * rows, rows)] = own_part(kind, m, c).astype(jnp.bfloat16)
            far_copy(kind, m, c).start()

    def give_sum(kind, c):
        place = pl.ds(pl.multiple_of(core * half + c * rows, rows), rows)
        return to_mate(
            sums.at[kind, place], sums.at[kind, place], give_sem, kind * CHUNKS + c, mate
        )

    def finish_sum(kind, totals):
        for c in range(CHUNKS):
            part = pl.ds(c * rows, rows)
            total = totals[c]
            for m in order[:-1]:
                far_copy(kind, m, c).wait_recv()
                total = total + far[kind, m, part].astype(jnp.float32)
            place = pl.ds(pl.multiple_of(core * half + c * rows, rows), rows)
            sums[kind, place] = total.astype(jnp.bfloat16)
            give_sum(kind, c).start()

    for m in order:
        for k in range(2):
            owner = aim(m) * 2 + (1 - inner if k == 0 else inner)
            slot = 2 * m + k
            first = flags_ref[shard * count + owner] == 1
            loads[slot].wait()
            swaps[slot].wait_recv()
            one, two = mine[slot], inbox[slot]
            mine[slot] = lax.select(first, one, two)
            inbox[slot] = lax.select(first, two, one)
            if k == 0:
                for c in range(CHUNKS):
                    near_copy(0, m, c).start()
    for m in order[:-1]:
        pass_on(0, m)
    totals = [own_part(0, 0, c) for c in range(CHUNKS)]
    for m in order:
        for c in range(CHUNKS):
            near_copy(1, m, c).start()
    finish_sum(0, totals)
    pass_on(1, order[0])

    for state in states[:2]:
        state.wait()
    give_stat.wait_recv()
    give_basis.wait_recv()
    held[...] = lax.select(listed, left_basis[...], mate_basis[...]).T
    for c in range(CHUNKS):
        give_sum(0, c).wait()
    grad = sums[0]
    rate = (1.0 - beta_two) / side
    turned[...] = (
        beta_two * lax.select(listed, left_stat[...], mate_stat[...])
        + rate * lax.select(listed, low_product(grad, grad, (1, 1)), low_product(grad, grad, (0, 0)))
    ).astype(jnp.bfloat16)
    for m in order[1:2]:
        pass_on(1, m)

    def give_turn(kind):
        return to_mate(fresh_turn.at[kind, given], mate_turn.at[kind], mate_sem, 2 + kind, mate)

    def along(kind, m, c):
        part = pl.ds(c * rows, rows)
        return to_replica(
            own_turn.at[kind, part],
            gathered.at[kind, me, part],
            along_sem,
            (kind, m, c),
            aim(m) * 2 + inner,
        )

    def across(kind, m, c):
        part = pl.ds(c * rows, rows)
        origin = lax.rem(outer - m + outer_count, outer_count) * 2 + inner
        source = own_turn.at[kind, part] if m == 0 else gathered.at[kind, origin, part]
        return to_replica(
            source, gathered.at[kind, origin, part], across_sem, (kind, m, c), partner
        )

    def start_turn(kind, choose):
        give_turn(kind).wait()
        own_turn[kind] = lax.select(choose, fresh_turn[kind, kept], mate_turn[kind])
        for c in range(CHUNKS):
            across(kind, 0, c).start()
        for m in closest:
            for c in range(CHUNKS):
                along(kind, m, c).start()

    def forward_turn(kind, m):
        for c in range(CHUNKS):
            along(kind, m, c).wait_recv()
            across(kind, m, c).start()

    def middle():
        for state in states[2:]:
            state.wait()
        for c in range(CHUNKS):
            give_sum(1, c).wait()
        own_sum[...] = lax.select(listed, sums[0], sums[1])
        low_left, low_right = left_basis[...].astype(jnp.bfloat16), right_basis[...].astype(jnp.bfloat16)
        fresh_turn[1] = moved(low_left, low_right, own_sum[...], moment[...], second[...])[2]
        give_turn(1).start()

    def restore():
        plain[...] = low_product(
            low_product(left_basis[...], moment[...]), right_basis[...], (1, 1)
        ).astype(jnp.bfloat16)

    def statistics():
        grad = own_sum[...]
        left_stat[...] = beta_two * left_stat[...] + rate * low_product(grad, grad, (1, 1))
        right_stat[...] = beta_two * right_stat[...] + rate * low_product(grad, grad, (0, 0))

    def store(index, source, target):
        return pltpu.make_async_copy(source, target.at[0], store_sem.at[index])

    refresh(
        held,
        joint,
        turned,
        (
            lambda: [pass_on(1, m) for m in order[2:-1]],
            lambda: None,
            lambda: None,
            lambda: [
                finish_sum(1, [own_part(1, 0, c) for c in range(CHUNKS)]),
                middle(),
                restore(),
                start_turn(1, jnp.logical_not(listed)),
            ],
            lambda: None,
            lambda: [forward_turn(1, m) for m in closest[:1]],
            lambda: [forward_turn(1, m) for m in closest[1:2]],
            lambda: None,
        ),
    )
    turned[...] = held[...].T.astype(jnp.bfloat16)
    give_turned = to_mate(turned, arrived, mate_sem, 4, mate)
    give_turned.start()
    left_basis[...] = lax.select(listed, held[...].T, left_basis[...])
    low_left = left_basis[...].astype(jnp.bfloat16)
    part_moment = low_product(low_left, plain[...], (0, 0))
    give_turned.wait()
    right_basis[...] = lax.select(listed, arrived[...].astype(jnp.float32), right_basis[...])
    low_right = right_basis[...].astype(jnp.bfloat16)
    carried = lax.select(listed, low_product(part_moment, low_right), moment[...])
    moment_new, second_new, turn = moved(
        low_left, low_right, own_sum[...], carried, second[...]
    )
    fresh_turn[0] = turn
    give_turn(0).start()
    for m in closest[2:]:
        forward_turn(1, m)
    start_turn(0, listed)
    moment[...] = moment_new
    second[...] = second_new
    statistics()
    ends = [
        store(0, left_stat, left_out),
        store(1, right_stat, right_out),
        store(2, moment, moment_out),
        store(3, second, second_out),
        store(4, left_basis, left_basis_out),
        store(5, right_basis, right_basis_out),
    ]
    for end in ends:
        end.start()
    for kind in range(2):
        for m in order:
            for c in range(CHUNKS):
                near_copy(kind, m, c).wait_send()
                if m:
                    far_copy(kind, m, c).wait_send()
    for swap in swaps.values():
        swap.wait_send()
    give_stat.wait_send()
    give_basis.wait_send()

    def keep_out(owner):
        return pltpu.make_async_copy(
            mine.at[owner], direction_out.at[owner, kept], out_sem.at[owner]
        )

    def give_out(owner):
        return to_mate(
            inbox.at[owner], direction_out.at[owner, kept], swap_sem, owner, mate
        )

    def assemble(owner, first, second_kind):
        flag = flags_ref[shard * count + owner] == 1
        mine[owner] = lax.select(flag, first, second_kind)
        inbox[owner] = lax.select(flag, second_kind, first)
        keep_out(owner).start()
        give_out(owner).start()

    assemble(me, own_turn[0], own_turn[1])
    for m in closest:
        forward_turn(0, m)
        origin = lax.rem(outer - m + outer_count, outer_count) * 2 + inner
        assemble(origin, gathered[0, origin], gathered[1, origin])
    for m in [0] + closest:
        origin = lax.rem(outer - m + outer_count, outer_count) * 2 + 1 - inner
        for kind in (1, 0):
            for c in range(CHUNKS):
                across(kind, m, c).wait_recv()
        assemble(origin, gathered[0, origin], gathered[1, origin])
    for kind in range(2):
        for m in order:
            for c in range(CHUNKS):
                across(kind, m, c).wait_send()
                if m:
                    along(kind, m, c).wait_send()
    for end in ends:
        end.wait()
    for owner in range(count):
        keep_out(owner).wait()
        give_out(owner).wait()


SMEM = pl.BlockSpec(memory_space=pltpu.SMEM)
ANY = pl.BlockSpec(memory_space=pl.ANY)
HBM = pl.BlockSpec(memory_space=pltpu.HBM)


def local(
    gradients,
    first_moment,
    second_moment,
    left_stat,
    right_stat,
    left_basis,
    right_basis,
    refresh_flags,
):
    count, side = gradients.shape[1], gradients.shape[2]
    outer, half = count // 2, side // 2
    wide = jax.ShapeDtypeStruct((1, side, side), jnp.float32)
    low = jax.ShapeDtypeStruct((count, side, side), jnp.bfloat16)

    def low_held(*shape):
        return pltpu.VMEM(shape, jnp.bfloat16)

    def flags(*shape):
        return pltpu.SemaphoreType.DMA(shape)

    block = pltpu.VMEM((side, side), jnp.float32)
    return pl.pallas_call(
        soap_kernel,
        out_shape=(low,) + (wide,) * 6,
        in_specs=[SMEM] + [HBM] * 7,
        out_specs=(ANY,) * 7,
        scratch_shapes=[
            low_held(count, half, side),
            low_held(count, half, side),
            low_held(2, outer, half, side),
            low_held(2, outer, half, side),
            low_held(2, outer, half, side),
            low_held(2, side, side),
            low_held(2, count, half, side),
            low_held(2, side, side),
            low_held(2, half, side),
            low_held(2, half, side),
        ]
        + [block] * 8
        + [low_held(side, side)] * 4
        + [block, pltpu.VMEM((side, 2 * side), jnp.float32)]
        + [
            flags(count),
            flags(6),
            flags(6),
            flags(count),
            flags(2, count),
            flags(2, 5),
            flags(2, 2 * CHUNKS),
            flags(2, 2, outer, CHUNKS),
            flags(2, 2, outer, CHUNKS),
            flags(2, 2, outer, CHUNKS),
            flags(2, 2, outer, CHUNKS),
        ],
        compiler_params=pltpu.CompilerParams(
            collective_id=0, has_side_effects=True, vmem_limit_bytes=60 << 20
        ),
        name="soap",
    )(
        refresh_flags,
        gradients,
        first_moment,
        second_moment,
        left_stat,
        right_stat,
        left_basis,
        right_basis,
    )


def solution(mesh):
    owned = P(("shard", "replica"), None, None)
    in_specs = (P("replica", "shard", None, None),) + (owned,) * 6 + (P(),)
    out_specs = (P("shard", None, None),) + (owned,) * 6
    return jax.shard_map(local, mesh=mesh, in_specs=in_specs, out_specs=out_specs, check_vma=False)
```

```python
import jax
import jax.numpy as jnp
from jax import lax
from jax.experimental import pallas as pl
from jax.experimental.pallas import tpu as pltpu
from jax.sharding import PartitionSpec as P

POWER = 2


beta_one = 0.95
beta_two = 0.95
epsilon = 1e-08
bias_step = 10.0

TILE = 128
ROWS = 8
CHUNKS = 4
MESH = pl.DeviceIdType.MESH


def product(left_side, right_side, contract=(1, 0), precision=lax.Precision.HIGHEST):
    return lax.dot_general(
        left_side,
        right_side,
        (((contract[0],), (contract[1],)), ((), ())),
        precision=precision,
        preferred_element_type=jnp.float32,
    )


def low_product(left_side, right_side, contract=(1, 0)):
    return product(
        left_side.astype(jnp.bfloat16), right_side.astype(jnp.bfloat16), contract, None
    )


HEAD = 16


def spread_lane(rows, at):
    return jnp.broadcast_to(rows[:, at : at + 1], rows.shape) + 0.0

def spread_row(rows, at):
    return jnp.broadcast_to(rows[at : at + 1, :], rows.shape)

def inverse_factor(tile):
    side = tile.shape[0]
    spread = (ROWS, side)
    lane = lax.broadcasted_iota(jnp.int32, spread, 1)
    sub = lax.broadcasted_iota(jnp.int32, spread, 0)
    parts = HEAD // ROWS
    count = side // HEAD
    groups = [tile[ROWS * g : ROWS * (g + 1), :] for g in range(side // ROWS)]
    finished = []
    for step in range(count):
        start = HEAD * step
        first = parts * step
        inside = (lane >= start) & (lane < start + HEAD)
        old = groups[first : first + parts]
        columns = [[spread_lane(rows, start + t) for rows in old] for t in range(HEAD)]
        lines = [
            jnp.where(inside, jnp.where(lane == start + ROWS * v + sub, 1.0, 0.0), old[v])
            for v in range(parts)
        ]
        done = [jnp.zeros(spread, jnp.float32)] * parts
        scale = [jnp.zeros(spread, jnp.float32)] * parts
        for j in range(HEAD):
            own, row = divmod(j, ROWS)
            here = sub == row
            pivot = spread_row(columns[j][own], row)
            inverse = 1.0 / pivot
            ratio = [column * inverse for column in columns[j]]
            ratio[own] = jnp.where(here, 0.0, ratio[own])
            for t in range(j + 1, HEAD):
                across = spread_row(columns[j][t // ROWS], t % ROWS)
                for v in range(parts):
                    if t == j + 1:
                        change = (columns[j][v] * across) * inverse
                        if v == own:
                            change = jnp.where(here, 0.0, change)
                    else:
                        change = ratio[v] * across
                    columns[t][v] = columns[t][v] - change
            line = spread_row(lines[own], row)
            done[own] = jnp.where(here, line * lax.rsqrt(pivot), done[own])
            scale[own] = jnp.where(here, inverse, scale[own])
            for v in range(parts):
                lines[v] = lines[v] - ratio[v] * line
        finished += [jnp.where(lane < start + HEAD, rows, 0.0) for rows in done]
        if step + 1 == count:
            break
        back = [lines[v] * scale[v] for v in range(parts)]
        edge = min(first + 2 * parts, side // ROWS)
        across = [spread_row(back[j // ROWS], j % ROWS) for j in range(HEAD)]
        for g in range(first + parts, edge):
            terms = [spread_lane(groups[g], start + j) * across[j] for j in range(HEAD)]
            while len(terms) > 1:
                terms = [terms[t] + terms[t + 1] for t in range(0, len(terms), 2)]
            groups[g] = jnp.where(inside, 0.0, groups[g]) - terms[0]
        if edge < side // ROWS:
            change = lax.dot_general(wide(jnp.concatenate(old, 0), 0), wide(jnp.concatenate(back, 0), 1), (((0,), (0,)), ((), ())), preferred_element_type=jnp.float32)
            for g in range(edge, side // ROWS):
                groups[g] = jnp.where(inside, 0.0, groups[g]) - change[ROWS * g : ROWS * (g + 1), :]
    return jnp.concatenate(finished, 0)

def wide(x, kind):
    a = x.astype(jnp.bfloat16); r = x - a.astype(jnp.float32); b = r.astype(jnp.bfloat16); c = (r - b.astype(jnp.float32)).astype(jnp.bfloat16)
    return jnp.concatenate([a, a, b, b, a, c] if kind == 0 else [a, b, a, b, c, a], 0)


def refresh(held, joint, turned, pauses):
    side = held.shape[0]
    steps, passed, pauses = POWER * (side // TILE), 0, list(pauses)
    spacing = len(pauses)
    for repeat in range(POWER):
        across = product(held[...].astype(jnp.bfloat16), turned[...], precision=None)
        joint[:, side:] = across
        joint[:, :side] = product(across, across, (1, 1))
        tile = joint[:TILE, :TILE]
        for block in range(side // TILE):
            at, after = block * TILE, (block + 1) * TILE
            inverse = inverse_factor(tile)
            if after < side:
                near = product(joint[after : after + TILE, at:after], inverse, (1, 1))
                tile = joint[after : after + TILE, after : after + TILE] - product(
                    near, near, (1, 1)
                )
            fresh = product(inverse, joint[at:after, side:])
            held[at:after, :] = fresh
            if after < side:
                joint[after : after + TILE, side:] -= product(near, fresh)
            if after + TILE < side:
                below = product(joint[after + TILE :, at:after], inverse, (1, 1))
                joint[after + TILE :, after : after + TILE] -= product(below, near, (1, 1))
                joint[after + TILE :, after + TILE : side] -= product(below, below, (1, 1))
                joint[after + TILE :, side:] -= product(below, fresh)
            passed += 1
            while pauses and (spacing - len(pauses) + 1) * steps <= passed * spacing:
                pauses.pop(0)()


def moved(left, right, grad, carried, second):
    rotated = low_product(low_product(left, grad, (0, 0)), right)
    moment_new = beta_one * carried + (1.0 - beta_one) * rotated
    second_new = beta_two * second + (1.0 - beta_two) * rotated * rotated
    scaled = (
        moment_new
        / (1.0 - beta_one**bias_step)
        / (jnp.sqrt(second_new / (1.0 - beta_two**bias_step)) + epsilon)
    )
    turn = low_product(low_product(left, scaled), right, (1, 1)).astype(jnp.bfloat16)
    return moment_new, second_new, turn


def sequence(outer_count):
    return sorted(range(outer_count), key=lambda m: (m == 0, abs(2 * m - outer_count), m))


def to_replica(source, target, sems, index, replica):
    return pltpu.make_async_remote_copy(
        src_ref=source,
        dst_ref=target,
        send_sem=sems.at[(0,) + index],
        recv_sem=sems.at[(1,) + index],
        device_id={"replica": replica},
        device_id_type=MESH,
    )


def to_mate(source, target, sems, index, mate):
    return pltpu.make_async_remote_copy(
        src_ref=source,
        dst_ref=target,
        send_sem=sems.at[0, index],
        recv_sem=sems.at[1, index],
        device_id={"shard": mate},
        device_id_type=MESH,
    )


def soap_kernel(
    flags_ref,
    grad_ref,
    moment_ref,
    second_ref,
    left_stat_ref,
    right_stat_ref,
    left_basis_ref,
    right_basis_ref,
    direction_out,
    moment_out,
    second_out,
    left_out,
    right_out,
    left_basis_out,
    right_basis_out,
    mine,
    inbox,
    got,
    pairs,
    far,
    sums,
    gathered,
    fresh_turn,
    mate_turn,
    own_turn,
    moment,
    second,
    left_stat,
    right_stat,
    left_basis,
    right_basis,
    mate_stat,
    mate_basis,
    own_sum,
    plain,
    turned,
    arrived,
    held,
    joint,
    load_sem,
    state_sem,
    store_sem,
    out_sem,
    swap_sem,
    mate_sem,
    give_sem,
    near_sem,
    far_sem,
    along_sem,
    across_sem,
):
    count, half, side = mine.shape
    outer_count = count // 2
    rows = half // CHUNKS
    me, shard = lax.axis_index("replica"), lax.axis_index("shard")
    core = lax.rem(shard, 2)
    mate = shard + 1 - 2 * core
    inner = lax.rem(me, 2)
    outer = me // 2
    partner = me + 1 - 2 * inner
    order = sequence(outer_count)
    closest = sorted(range(1, outer_count), key=lambda m: min(m, outer_count - m))
    listed = flags_ref[shard * count + me] == 1
    kept = pl.ds(pl.multiple_of(core * half, half), half)
    given = pl.ds(pl.multiple_of((1 - core) * half, half), half)

    def aim(m):
        return lax.rem(outer + m, outer_count)

    barrier = pltpu.get_barrier_semaphore()
    pl.semaphore_signal(barrier, inc=1, device_id={"shard": mate}, device_id_type=MESH)
    pl.semaphore_signal(barrier, inc=1, device_id={"replica": partner}, device_id_type=MESH)
    for m in range(1, outer_count):
        pl.semaphore_signal(
            barrier, inc=1, device_id={"replica": aim(m) * 2 + inner}, device_id_type=MESH
        )
    pl.semaphore_wait(barrier, outer_count + 1)

    swaps, loads = {}, {}
    for m in order:
        for k in range(2):
            owner = aim(m) * 2 + (1 - inner if k == 0 else inner)
            slot = 2 * m + k
            swaps[slot] = to_mate(
                grad_ref.at[0, owner, given], inbox.at[slot], swap_sem, slot, mate
            )
            swaps[slot].start()
            loads[slot] = pltpu.make_async_copy(
                grad_ref.at[0, owner, kept], mine.at[slot], load_sem.at[slot]
            )
            loads[slot].start()
    give_stat = to_mate(right_stat_ref.at[0], mate_stat, mate_sem, 0, mate)
    give_basis = to_mate(right_basis_ref.at[0], mate_basis, mate_sem, 1, mate)
    give_stat.start()
    give_basis.start()
    states = []
    for index, (source, target) in enumerate(
        [
            (left_stat_ref, left_stat),
            (left_basis_ref, left_basis),
            (right_stat_ref, right_stat),
            (right_basis_ref, right_basis),
            (moment_ref, moment),
            (second_ref, second),
        ]
    ):
        states.append(pltpu.make_async_copy(source.at[0], target, state_sem.at[index]))
        states[-1].start()

    def near_copy(kind, m, c):
        part = pl.ds(c * rows, rows)
        source = (mine, inbox)[kind].at[2 * m, part]
        return to_replica(source, got.at[kind, m, part], near_sem, (kind, m, c), partner)

    def far_copy(kind, m, c):
        part = pl.ds(c * rows, rows)
        return to_replica(
            pairs.at[kind, m, part],
            far.at[kind, m, part],
            far_sem,
            (kind, m, c),
            aim(m) * 2 + inner,
        )

    def own_part(kind, m, c):
        part = pl.ds(c * rows, rows)
        near_copy(kind, m, c).wait_recv()
        stay = (mine, inbox)[kind][2 * m + 1, part]
        return stay.astype(jnp.float32) + got[kind, m, part].astype(jnp.float32)

    def pass_on(kind, m):
        for c in range(CHUNKS):
            pairs[kind, m, pl.ds(c * rows, rows)] = own_part(kind, m, c).astype(jnp.bfloat16)
            far_copy(kind, m, c).start()

    def give_sum(kind, c):
        place = pl.ds(pl.multiple_of(core * half + c * rows, rows), rows)
        return to_mate(
            sums.at[kind, place], sums.at[kind, place], give_sem, kind * CHUNKS + c, mate
        )

    def finish_sum(kind, totals):
        for c in range(CHUNKS):
            part = pl.ds(c * rows, rows)
            total = totals[c]
            for m in order[:-1]:
                far_copy(kind, m, c).wait_recv()
                total = total + far[kind, m, part].astype(jnp.float32)
            place = pl.ds(pl.multiple_of(core * half + c * rows, rows), rows)
            sums[kind, place] = total.astype(jnp.bfloat16)
            give_sum(kind, c).start()

    for m in order:
        for k in range(2):
            owner = aim(m) * 2 + (1 - inner if k == 0 else inner)
            slot = 2 * m + k
            first = flags_ref[shard * count + owner] == 1
            loads[slot].wait()
            swaps[slot].wait_recv()
            one, two = mine[slot], inbox[slot]
            mine[slot] = lax.select(first, one, two)
            inbox[slot] = lax.select(first, two, one)
            if k == 0:
                for c in range(CHUNKS):
                    near_copy(0, m, c).start()
    for m in order[:-1]:
        pass_on(0, m)
    totals = [own_part(0, 0, c) for c in range(CHUNKS)]
    for m in order:
        for c in range(CHUNKS):
            near_copy(1, m, c).start()
    finish_sum(0, totals)

    for state in states[:2]:
        state.wait()
    give_stat.wait_recv()
    give_basis.wait_recv()
    held[...] = lax.select(listed, left_basis[...], mate_basis[...]).T
    for c in range(CHUNKS):
        give_sum(0, c).wait()
    grad = sums[0]
    rate = (1.0 - beta_two) / side
    turned[...] = (
        beta_two * lax.select(listed, left_stat[...], mate_stat[...])
        + rate * lax.select(listed, low_product(grad, grad, (1, 1)), low_product(grad, grad, (0, 0)))
    ).astype(jnp.bfloat16)
    pass_on(1, order[0])

    def give_turn(kind):
        return to_mate(fresh_turn.at[kind, given], mate_turn.at[kind], mate_sem, 2 + kind, mate)

    def along(kind, m, c):
        part = pl.ds(c * rows, rows)
        return to_replica(
            own_turn.at[kind, part],
            gathered.at[kind, me, part],
            along_sem,
            (kind, m, c),
            aim(m) * 2 + inner,
        )

    def across(kind, m, c):
        part = pl.ds(c * rows, rows)
        origin = lax.rem(outer - m + outer_count, outer_count) * 2 + inner
        source = own_turn.at[kind, part] if m == 0 else gathered.at[kind, origin, part]
        return to_replica(
            source, gathered.at[kind, origin, part], across_sem, (kind, m, c), partner
        )

    def start_turn(kind, choose):
        give_turn(kind).wait()
        own_turn[kind] = lax.select(choose, fresh_turn[kind, kept], mate_turn[kind])
        for c in range(CHUNKS):
            across(kind, 0, c).start()
        for m in closest:
            for c in range(CHUNKS):
                along(kind, m, c).start()

    def forward_turn(kind, m):
        for c in range(CHUNKS):
            along(kind, m, c).wait_recv()
            across(kind, m, c).start()

    def middle():
        for state in states[2:]:
            state.wait()
        for c in range(CHUNKS):
            give_sum(1, c).wait()
        own_sum[...] = lax.select(listed, sums[0], sums[1])
        low_left, low_right = left_basis[...].astype(jnp.bfloat16), right_basis[...].astype(jnp.bfloat16)
        fresh_turn[1] = moved(low_left, low_right, own_sum[...], moment[...], second[...])[2]
        give_turn(1).start()

    def restore():
        plain[...] = low_product(
            low_product(left_basis[...], moment[...]), right_basis[...], (1, 1)
        ).astype(jnp.bfloat16)

    def statistics():
        grad = own_sum[...]
        left_stat[...] = beta_two * left_stat[...] + rate * low_product(grad, grad, (1, 1))
        right_stat[...] = beta_two * right_stat[...] + rate * low_product(grad, grad, (0, 0))

    def store(index, source, target):
        return pltpu.make_async_copy(source, target.at[0], store_sem.at[index])

    refresh(
        held,
        joint,
        turned,
        (
            lambda: [pass_on(1, m) for m in order[1:2]],
            lambda: [pass_on(1, m) for m in order[2:-1]],
            lambda: None,
            lambda: [
                finish_sum(1, [own_part(1, 0, c) for c in range(CHUNKS)]),
                middle(),
                restore(),
                start_turn(1, jnp.logical_not(listed)),
            ],
            lambda: None,
            lambda: [forward_turn(1, m) for m in closest[:1]],
            lambda: [forward_turn(1, m) for m in closest[1:2]],
            lambda: None,
        ),
    )
    turned[...] = held[...].T.astype(jnp.bfloat16)
    give_turned = to_mate(turned, arrived, mate_sem, 4, mate)
    give_turned.start()
    left_basis[...] = lax.select(listed, held[...].T, left_basis[...])
    low_left = left_basis[...].astype(jnp.bfloat16)
    part_moment = low_product(low_left, plain[...], (0, 0))
    give_turned.wait()
    right_basis[...] = lax.select(listed, arrived[...].astype(jnp.float32), right_basis[...])
    low_right = right_basis[...].astype(jnp.bfloat16)
    carried = lax.select(listed, low_product(part_moment, low_right), moment[...])
    moment_new, second_new, turn = moved(
        low_left, low_right, own_sum[...], carried, second[...]
    )
    fresh_turn[0] = turn
    give_turn(0).start()
    for m in closest[2:]:
        forward_turn(1, m)
    start_turn(0, listed)
    moment[...] = moment_new
    second[...] = second_new
    statistics()
    ends = [
        store(0, left_stat, left_out),
        store(1, right_stat, right_out),
        store(2, moment, moment_out),
        store(3, second, second_out),
        store(4, left_basis, left_basis_out),
        store(5, right_basis, right_basis_out),
    ]
    for end in ends:
        end.start()
    for kind in range(2):
        for m in order:
            for c in range(CHUNKS):
                near_copy(kind, m, c).wait_send()
                if m:
                    far_copy(kind, m, c).wait_send()
    for swap in swaps.values():
        swap.wait_send()
    give_stat.wait_send()
    give_basis.wait_send()

    def keep_out(owner):
        return pltpu.make_async_copy(
            mine.at[owner], direction_out.at[owner, kept], out_sem.at[owner]
        )

    def give_out(owner):
        return to_mate(
            inbox.at[owner], direction_out.at[owner, kept], swap_sem, owner, mate
        )

    def assemble(owner, first, second_kind):
        flag = flags_ref[shard * count + owner] == 1
        mine[owner] = lax.select(flag, first, second_kind)
        inbox[owner] = lax.select(flag, second_kind, first)
        keep_out(owner).start()
        give_out(owner).start()

    assemble(me, own_turn[0], own_turn[1])
    for m in closest:
        forward_turn(0, m)
        origin = lax.rem(outer - m + outer_count, outer_count) * 2 + inner
        assemble(origin, gathered[0, origin], gathered[1, origin])
    for m in [0] + closest:
        origin = lax.rem(outer - m + outer_count, outer_count) * 2 + 1 - inner
        for kind in (1, 0):
            for c in range(CHUNKS):
                across(kind, m, c).wait_recv()
        assemble(origin, gathered[0, origin], gathered[1, origin])
    for kind in range(2):
        for m in order:
            for c in range(CHUNKS):
                across(kind, m, c).wait_send()
                if m:
                    along(kind, m, c).wait_send()
    for end in ends:
        end.wait()
    for owner in range(count):
        keep_out(owner).wait()
        give_out(owner).wait()


SMEM = pl.BlockSpec(memory_space=pltpu.SMEM)
ANY = pl.BlockSpec(memory_space=pl.ANY)
HBM = pl.BlockSpec(memory_space=pltpu.HBM)


def local(
    gradients,
    first_moment,
    second_moment,
    left_stat,
    right_stat,
    left_basis,
    right_basis,
    refresh_flags,
):
    count, side = gradients.shape[1], gradients.shape[2]
    outer, half = count // 2, side // 2
    wide = jax.ShapeDtypeStruct((1, side, side), jnp.float32)
    low = jax.ShapeDtypeStruct((count, side, side), jnp.bfloat16)

    def low_held(*shape):
        return pltpu.VMEM(shape, jnp.bfloat16)

    def flags(*shape):
        return pltpu.SemaphoreType.DMA(shape)

    block = pltpu.VMEM((side, side), jnp.float32)
    return pl.pallas_call(
        soap_kernel,
        out_shape=(low,) + (wide,) * 6,
        in_specs=[SMEM] + [HBM] * 7,
        out_specs=(ANY,) * 7,
        scratch_shapes=[
            low_held(count, half, side),
            low_held(count, half, side),
            low_held(2, outer, half, side),
            low_held(2, outer, half, side),
            low_held(2, outer, half, side),
            low_held(2, side, side),
            low_held(2, count, half, side),
            low_held(2, side, side),
            low_held(2, half, side),
            low_held(2, half, side),
        ]
        + [block] * 8
        + [low_held(side, side)] * 4
        + [block, pltpu.VMEM((side, 2 * side), jnp.float32)]
        + [
            flags(count),
            flags(6),
            flags(6),
            flags(count),
            flags(2, count),
            flags(2, 5),
            flags(2, 2 * CHUNKS),
            flags(2, 2, outer, CHUNKS),
            flags(2, 2, outer, CHUNKS),
            flags(2, 2, outer, CHUNKS),
            flags(2, 2, outer, CHUNKS),
        ],
        compiler_params=pltpu.CompilerParams(
            collective_id=0, has_side_effects=True, vmem_limit_bytes=60 << 20
        ),
        name="soap",
    )(
        refresh_flags,
        gradients,
        first_moment,
        second_moment,
        left_stat,
        right_stat,
        left_basis,
        right_basis,
    )


def solution(mesh):
    owned = P(("shard", "replica"), None, None)
    in_specs = (P("replica", "shard", None, None),) + (owned,) * 6 + (P(),)
    out_specs = (P("shard", None, None),) + (owned,) * 6
    return jax.shard_map(local, mesh=mesh, in_specs=in_specs, out_specs=out_specs, check_vma=False)
```
